32 devices in a mesh: batch: 8 (over z, x), owner: 4 (over y, core).
Axes of the slice: x: 2, y: 2, z: 4, core: 2. Of those that a mesh axis runs over, the one named last changes fastest.
Arguments:
- queries: bfloat16 [128, 32, 128], P(('batch', 'owner')), may hold values from -8 to 8
- pool: bfloat16 [32, 184, 128], P(('owner', 'batch')), may hold values from -20 to 20
- lengths: int32 [32], P('owner'), may hold values from 46 to 180, as said below
- candidates: int32 [128, 12], P('batch'), may hold values from 0 to 31, as said below
- owner_map: int32 [32], replicated, may hold values from 0 to 31, as said below
- teacher: float32 [128, 12], P(('batch', 'owner')), may hold values from -12 to 12
Outputs:
- query_grad: float32 [128, 32, 128], P(('batch', 'owner'))
- divergence: float32 [128], P(('batch', 'owner'))
The draws below stay inside these ranges and needn't reach their ends.
Inputs may be any that keep to these rules, and one draw needn't show every extreme that they name: `lengths`: every owner group (pool rows k * 8 to (k + 1) * 8 - 1) holds a passage of exactly 180 tokens. `owner_map`: A permutation: each pool row belongs to one passage id. Each query names 12 different passages. The owner group of a passage p is owner_map[p] // 8. All queries of one batch index have the same number of candidates in each owner group: 6 in some of the groups, 3 in half, none in a quarter; which groups these are differs between batch indices.
All inputs are finite; a program needn't handle non-finite values.
Results may differ from the reference program's by a relative error of at most 0.0075.
Values may be sent and summed in bfloat16 or wider, within the bound.
No kernel may reach another device: no remote copies, remote signals or barrier semaphores. Data moves between devices by JAX's collectives and lax.ppermute only.
A program may use at most 64 MiB of HBM per device.

```python
import math
import jax
import jax.numpy as jnp
from jax import lax

D = 128
QLEN = 32
MAXLEN = 180
PLEN = 184
CPO = 3
NQ = 128
ROWQ = 16
P_OWN = 8
NP = 32
NCAND = 12
HOT = 6
N_BATCH = 8
N_OWNER = 4


def slot_table(key):
    return jax.random.permutation(jax.random.fold_in(key, 21), NP).astype(jnp.int32)


def draw_owner_map(key, part):
    return slot_table(key)


def draw_lengths(key, part):
    shortest = MAXLEN // 4 + 1
    values = jax.random.randint(jax.random.fold_in(key, 11), (N_OWNER, P_OWN), shortest, MAXLEN + 1)
    longest_at = jax.random.randint(jax.random.fold_in(key, 12), (N_OWNER, 1), 0, P_OWN)
    is_longest = jnp.arange(P_OWN)[None, :] == longest_at
    return jnp.where(is_longest, MAXLEN, values).reshape(NP).astype(jnp.int32)


def draw_candidates(key, part):
    slots_of = slot_table(key)
    passage_of = jnp.argsort(slots_of).astype(jnp.int32)
    quarter = N_OWNER // 4
    owner_idx = jnp.arange(N_OWNER)
    profile = jnp.where(owner_idx < quarter, 2 * CPO, jnp.where(owner_idx < 3 * quarter, CPO, 0))
    order_scores = jax.random.randint(jax.random.fold_in(key, 31), (N_BATCH, N_OWNER), 0, 1 << 20) * N_OWNER + owner_idx[None, :]
    owner_rank = jnp.argsort(jnp.argsort(order_scores, axis=1), axis=1)
    counts = profile[owner_rank]
    pick_scores = jax.random.randint(jax.random.fold_in(key, 32), (N_BATCH, ROWQ, N_OWNER, P_OWN), 0, 1 << 20) * P_OWN + jnp.arange(P_OWN)
    local_order = jnp.argsort(pick_scores, axis=-1)[..., :HOT]
    is_live = jnp.arange(HOT)[None, None, None, :] < counts[:, None, :, None]
    is_live = jnp.broadcast_to(is_live, (N_BATCH, ROWQ, N_OWNER, HOT))
    slot_full = owner_idx[None, None, :, None] * P_OWN + local_order
    width_all = N_OWNER * HOT
    flat_slot = slot_full.reshape(N_BATCH, ROWQ, width_all)
    flat_live = is_live.reshape(N_BATCH, ROWQ, width_all)
    mixing = jax.random.randint(jax.random.fold_in(key, 33), (N_BATCH, ROWQ, width_all), 0, 1 << 20) * width_all + jnp.arange(width_all)
    sort_key = mixing + jnp.where(flat_live, 0, 1 << 30)
    chosen_order = jnp.argsort(sort_key, axis=-1)[..., :NCAND]
    chosen = jnp.take_along_axis(flat_slot, chosen_order, axis=-1)
    return passage_of[chosen].reshape(NQ, NCAND).astype(jnp.int32)


def draw_queries(key, part):
    base = jnp.clip(jax.random.normal(jax.random.fold_in(key, 41), (NQ, QLEN, D), jnp.float32), -4.0, 4.0)
    spread = jax.random.uniform(jax.random.fold_in(key, 42), (NQ, QLEN, 1), jnp.float32, 0.0, 2.303)
    columns = jax.random.uniform(jax.random.fold_in(key, 43), (1, 1, D), jnp.float32, 0.0, 2.303)
    return (0.02 * base * jnp.exp(spread) * jnp.exp(columns)).astype(jnp.bfloat16)


def draw_pool(key, part):
    base = jnp.clip(jax.random.normal(jax.random.fold_in(key, 51), (NP, PLEN, D), jnp.float32), -4.0, 4.0)
    spread = jax.random.uniform(jax.random.fold_in(key, 52), (NP, PLEN, 1), jnp.float32, 0.0, 2.303)
    columns = jax.random.uniform(jax.random.fold_in(key, 53), (1, 1, D), jnp.float32, 0.0, 2.303)
    return (0.05 * base * jnp.exp(spread) * jnp.exp(columns)).astype(jnp.bfloat16)


def levels(rng, dims, shards, least, high):
    gain = 1.0
    for position, blocks in shards:
        draws = jax.random.uniform(jax.random.fold_in(jax.random.fold_in(rng, 6), position), (blocks,), jnp.float32, least / len(shards), high / len(shards))
        gain = gain * jnp.repeat(jnp.exp(draws), dims[position] // blocks).reshape((-1,) + (1,) * (len(dims) - 1 - position))
    return gain


def gaussian(rng, shape, scale, reach, pieces=(), dtype=jnp.bfloat16):
    result = scale * jax.random.normal(rng, shape, jnp.float32)
    if pieces:
        result = result * levels(rng, shape, pieces, -0.22, 0.18)
    return jnp.clip(result, -reach, reach).astype(dtype)


def setup_inputs(seed: int = 0) -> dict:
    key_list = jax.random.split(jax.random.key(seed), 7)
    queries = draw_queries(jax.random.fold_in(key_list[6], 71), 0)
    pool = draw_pool(jax.random.fold_in(key_list[6], 71), 0)
    lengths = draw_lengths(jax.random.fold_in(key_list[6], 71), 0)
    candidates = draw_candidates(jax.random.fold_in(key_list[6], 71), 0)
    owner_map = draw_owner_map(jax.random.fold_in(key_list[6], 71), 0)
    teacher = gaussian(key_list[5], (NQ, NCAND), 2.0, 12.0, ((0, 32),), jnp.float32)
    return {"queries": queries, "pool": pool, "lengths": lengths, "candidates": candidates, "owner_map": owner_map, "teacher": teacher}


SHARPNESS = 20.0
STUDENT_GAIN = 2.0
LOSS_SCALE = 64.0
EPSILON = 1e-06

def unit_rows(values):
    widened = values.astype(jnp.float32)
    inv_norm = lax.rsqrt(lax.optimization_barrier(jnp.sum(widened * widened, axis=-1, keepdims=True)) + EPSILON)
    return (widened * inv_norm, inv_norm)

def token_terms(query_block, passages, length_block):
    similar = jnp.einsum('bid,bktd->bkit', query_block.astype(jnp.float32), passages.astype(jnp.float32), precision=lax.Precision.HIGHEST)
    in_range = lax.broadcasted_iota(jnp.int32, similar.shape, 3) < length_block[:, :, None, None]
    exp_terms = jnp.where(in_range, jnp.exp(SHARPNESS * similar), 0.0)
    return (exp_terms, lax.optimization_barrier(jnp.sum(exp_terms, axis=3)))

def loss_terms(scores, teacher_rows):
    student = STUDENT_GAIN * scores
    log_student = student - jnp.log(lax.optimization_barrier(jnp.sum(jnp.exp(student), axis=1, keepdims=True)))
    log_target = teacher_rows - jnp.log(lax.optimization_barrier(jnp.sum(jnp.exp(teacher_rows), axis=1, keepdims=True)))
    target = jnp.exp(log_target)
    divergence = lax.optimization_barrier(jnp.sum(target * (log_target - log_student), axis=1))
    score_grad = LOSS_SCALE * STUDENT_GAIN * (jnp.exp(log_student) - target)
    return (divergence, score_grad)

def reference(queries, pool, lengths, candidates, owner_map, teacher):
    unit_query, inv_norm = unit_rows(queries)
    sent_query = unit_query.astype(jnp.bfloat16)
    cached = unit_rows(pool)[0].astype(jnp.bfloat16)
    slot_ids = jnp.take(owner_map, candidates, axis=0).astype(jnp.int32)
    length_of = jnp.take(lengths, slot_ids, axis=0).astype(jnp.int32)
    block_rows = math.gcd(NQ, 16)
    blocks = NQ // block_rows
    query_blocks = sent_query.reshape(blocks, block_rows, QLEN, D)
    slot_blocks = slot_ids.reshape(blocks, block_rows, NCAND)
    length_blocks = length_of.reshape(blocks, block_rows, NCAND)

    def forward(inputs):
        query_block, slot_block, length_block = inputs
        passages = jnp.take(cached, slot_block, axis=0)
        totals = token_terms(query_block, passages, length_block)[1]
        ratio = totals / length_block[:, :, None].astype(jnp.float32)
        return lax.optimization_barrier(jnp.sum(jnp.log(ratio), axis=2)) / SHARPNESS
    scores = lax.map(forward, (query_blocks, slot_blocks, length_blocks)).reshape(NQ, NCAND)
    divergence, score_grad = loss_terms(scores, teacher)
    grad_blocks = score_grad.reshape(blocks, block_rows, NCAND)

    def backward(inputs):
        query_block, slot_block, length_block, grad_block = inputs
        passages = jnp.take(cached, slot_block, axis=0)
        exp_terms, totals = token_terms(query_block, passages, length_block)
        weights = (exp_terms / totals[:, :, :, None]).astype(jnp.bfloat16)
        mixed = jnp.einsum('bkit,bktd->bkid', weights.astype(jnp.float32), passages.astype(jnp.float32), precision=lax.Precision.HIGHEST)
        return jnp.einsum('bk,bkid->bid', grad_block, mixed, precision=lax.Precision.HIGHEST)
    unit_grad = lax.map(backward, (query_blocks, slot_blocks, length_blocks, grad_blocks)).reshape(NQ, QLEN, D)
    radial = lax.optimization_barrier(jnp.sum(unit_query * unit_grad, axis=-1, keepdims=True))
    query_grad = (unit_grad - unit_query * radial) * inv_norm
    return (query_grad, divergence)
```

```python
import functools
import math

import jax
import jax.numpy as jnp
from jax import lax
from jax.experimental import pallas as pl
from jax.experimental.pallas import tpu as pltpu
from jax.sharding import PartitionSpec as P

SHARPNESS = 20.0
STUDENT_GAIN = 2.0
LOSS_SCALE = 64.0
EPSILON = 1e-06
LOG2E = math.log2(math.e)


VMEM_BUDGET = 24 << 20
VMEM = pl.BlockSpec(memory_space=pltpu.VMEM)
SMEM = pl.BlockSpec(memory_space=pltpu.SMEM)


def norm_kernel(where_ref, lengths_ref, pool_ref, out_ref):
    rows = pool_ref.shape[1]
    widened = pool_ref[0].astype(jnp.float32)
    inv = lax.rsqrt(jnp.sum(widened * widened, axis=-1, keepdims=True) + EPSILON)
    length = lengths_ref[where_ref[1]].astype(jnp.float32)
    last = lax.broadcasted_iota(jnp.int32, widened.shape, 0) == rows - 1
    out_ref[0] = jnp.where(last, length, widened * inv).astype(jnp.bfloat16)


def prep_kernel(n_rows, where_ref, cand_ref, map_ref, teacher_ref, query_ref,
                unit_ref, sent_ref, inv_ref, live_ref, target_ref, base_ref):
    own, toks, feat = query_ref.shape
    lanes = own * toks
    qt = query_ref[...].reshape(lanes, feat).astype(jnp.float32).T
    inv = lax.rsqrt(jnp.sum(qt * qt, axis=0, keepdims=True) + EPSILON)
    unit = qt * inv
    unit_ref[...] = unit
    sent_ref[...] = unit.astype(jnp.bfloat16)
    inv_ref[...] = inv
    ncand = cand_ref.shape[1]
    first = where_ref[0] * own
    me = where_ref[2]
    query_of = lax.broadcasted_iota(jnp.int32, (1, lanes), 1) // toks

    def spread(values):
        row = jnp.full((1, lanes), values[-1])
        for q in range(own - 1):
            row = jnp.where(query_of == q, values[q], row)
        return row

    def teacher_row(k):
        return spread([teacher_ref[q, k] for q in range(own)])

    total = jnp.zeros((1, lanes), jnp.float32)
    for k in range(ncand):
        total += jnp.exp(teacher_row(k))
    log_total = jnp.log(total)
    number = lax.broadcasted_iota(jnp.int32, (n_rows, lanes), 0)
    live = jnp.zeros((n_rows, lanes), jnp.float32)
    target = jnp.zeros((n_rows, lanes), jnp.float32)
    base = jnp.zeros((1, lanes), jnp.float32)
    mass = jnp.zeros((1, lanes), jnp.float32)
    for k in range(ncand):
        log_target = teacher_row(k) - log_total
        share = jnp.exp(log_target)
        base += share * log_target
        mass += share
        slot = spread([map_ref[cand_ref[first + q, k]] ^ me for q in range(own)])
        hit = number == slot
        live = jnp.where(hit, 1.0, live)
        target = jnp.where(hit, share, target)
    live_ref[...] = live
    target_ref[...] = target
    base_ref[0:1, :] = base
    base_ref[1:2, :] = mass


def score_kernel(deltas, toks, unit_ref, sent_ref, inv_ref, live_ref, target_ref, base_ref, *refs):
    pieces = refs[: len(deltas)]
    grad_ref, div_ref, e_ref, tot_ref, cnt_ref, acc_ref = refs[len(deltas):]
    rows, lanes = e_ref.shape[1:]
    feat = sent_ref.shape[0]
    sent = sent_ref[...]
    token = lax.broadcasted_iota(jnp.int32, (rows, lanes), 0).astype(jnp.float32)

    for ref, offs in zip(pieces, deltas):
        for i, delta in enumerate(offs):
            block = ref[i]
            length = block[rows - 8:, :].astype(jnp.float32)[7:8, :]
            similar = jnp.dot(block, sent, preferred_element_type=jnp.float32)
            terms = jnp.where(token < length, jnp.exp2(similar * (SHARPNESS * LOG2E)), 0.0)
            e_ref[delta] = terms
            tot_ref[delta:delta + 1, :] = jnp.sum(terms, axis=0, keepdims=True)
            cnt_ref[delta:delta + 1, :] = length

    totals = tot_ref[...]
    logs = jnp.log(totals / cnt_ref[...])
    same = (lax.broadcasted_iota(jnp.int32, (lanes, lanes), 0) // toks
            == lax.broadcasted_iota(jnp.int32, (lanes, lanes), 1) // toks).astype(jnp.float32)
    scores = jnp.dot(logs, same, precision=lax.Precision.HIGHEST, preferred_element_type=jnp.float32) / SHARPNESS
    student = STUDENT_GAIN * scores
    live = live_ref[...]
    target = target_ref[...]
    weight = live * jnp.exp(student)
    z = jnp.sum(weight, axis=0, keepdims=True)
    div = base_ref[0:1, :] - jnp.sum(target * student, axis=0, keepdims=True) + base_ref[1:2, :] * jnp.log(z)
    grad = LOSS_SCALE * STUDENT_GAIN * (weight / z - target)
    cnt_ref[...] = grad
    tot_ref[...] = 1.0 / totals

    acc_ref[...] = jnp.zeros_like(acc_ref)
    for ref, offs in zip(pieces, deltas):
        for i, delta in enumerate(offs):
            weights = (e_ref[delta] * tot_ref[delta:delta + 1, :]).astype(jnp.bfloat16)
            mixed = lax.dot_general(ref[i], weights, (((0,), (0,)), ((), ())), preferred_element_type=jnp.float32)
            acc_ref[...] += mixed * cnt_ref[delta:delta + 1, :]

    unit_grad = acc_ref[...]
    unit = unit_ref[...]
    radial = jnp.sum(unit * unit_grad, axis=0, keepdims=True)
    out = (unit_grad - unit * radial) * inv_ref[...]
    grad_ref[...] = out.T
    div_ref[...] = div


def exchange(value, axes, masks):
    sizes = [lax.axis_size(a) for a in axes]
    total = math.prod(sizes)

    def partner(i):
        out, rest = 0, i
        places = []
        for size in reversed(sizes):
            places.append(rest % size)
            rest //= size
        for place, size, mask in zip(reversed(places), sizes, masks):
            out = out * size + (place ^ mask)
        return out

    return lax.ppermute(value, axes if len(axes) > 1 else axes[0], [(i, partner(i)) for i in range(total)])


def gather_pool(block):
    nb, no = lax.axis_size("batch"), lax.axis_size("owner")
    held, offs = block, [0]
    for bit in range(1, nb.bit_length() - 1):
        held = jnp.concatenate([held, exchange(held, ("batch",), (1 << bit,))], axis=0)
        offs = offs + [d ^ (1 << bit) for d in offs]
    for bit in range(2, no.bit_length() - 1):
        held = jnp.concatenate([held, exchange(held, ("owner",), (1 << bit,))], axis=0)
        offs = offs + [d ^ (nb << bit) for d in offs]
    pieces = [(held, offs)]
    pieces.append((exchange(held, ("batch",), (1,)), [d ^ 1 for d in offs]))
    pieces.append((exchange(held, ("owner",), (2,)), [d ^ (2 * nb) for d in offs]))
    pieces.append((exchange(held, ("batch", "owner"), (1, 2)), [d ^ (2 * nb) ^ 1 for d in offs]))
    return pieces + [(exchange(v, ("owner",), (1,)), [d ^ nb for d in o]) for v, o in pieces]


def unit_rows(values):
    widened = values.astype(jnp.float32)
    inv_norm = lax.rsqrt(jnp.sum(widened * widened, axis=-1, keepdims=True) + EPSILON)
    return (widened * inv_norm, inv_norm)


def token_terms(query_block, passages, length_block):
    similar = jnp.einsum(
        "bid,bktd->bkit", query_block, passages, preferred_element_type=jnp.float32
    )
    in_range = lax.broadcasted_iota(jnp.int32, similar.shape, 3) < length_block[:, :, None, None]
    exp_terms = jnp.where(in_range, jnp.exp(SHARPNESS * similar), 0.0)
    return (exp_terms, jnp.sum(exp_terms, axis=3))


def loss_terms(scores, teacher_rows):
    student = STUDENT_GAIN * scores
    log_student = student - jnp.log(jnp.sum(jnp.exp(student), axis=1, keepdims=True))
    log_target = teacher_rows - jnp.log(jnp.sum(jnp.exp(teacher_rows), axis=1, keepdims=True))
    target = jnp.exp(log_target)
    divergence = jnp.sum(target * (log_target - log_student), axis=1)
    score_grad = LOSS_SCALE * STUDENT_GAIN * (jnp.exp(log_student) - target)
    return (divergence, score_grad)


def local_by_owner(queries, pool, lengths, candidates, owner_map, teacher):
    own_rows = queries.shape[0]
    all_rows = candidates.shape[0]
    tok_count = queries.shape[1]
    feature = queries.shape[2]
    slot_cap = 2 * (candidates.shape[1] // lax.axis_size("owner"))
    my_group = lax.axis_index("owner")
    unit_query, inv_norm = unit_rows(queries)
    sent_query = unit_query.astype(jnp.bfloat16)
    gathered = lax.all_gather(sent_query, "owner", axis=0, tiled=True)
    shard_unit = unit_rows(pool)[0].astype(jnp.bfloat16)
    cached = lax.all_gather(shard_unit, "batch", axis=0, tiled=True)
    group_rows = cached.shape[0]
    slot_ids = jnp.take(owner_map, candidates, axis=0)
    local_slot = slot_ids - my_group * group_rows
    is_local = (local_slot >= 0) & (local_slot < group_rows)
    order_rank = jnp.cumsum(is_local.astype(jnp.int32), axis=1) - 1
    slot_iota = lax.broadcasted_iota(jnp.int32, (1, 1, slot_cap), 2)
    matches = is_local[:, :, None] & (order_rank[:, :, None] == slot_iota)
    filled = jnp.any(matches, axis=1)
    pick_slot = jnp.sum(jnp.where(matches, local_slot[:, :, None], 0), axis=1)
    length_of = jnp.where(filled, jnp.take(lengths, pick_slot, axis=0), 1)

    def block_inputs(first_row, row_span):
        query_block = lax.dynamic_slice_in_dim(gathered, first_row, row_span, 0)
        pick_block = lax.dynamic_slice_in_dim(pick_slot, first_row, row_span, 0)
        length_block = lax.dynamic_slice_in_dim(length_of, first_row, row_span, 0)
        return (query_block, jnp.take(cached, pick_block, axis=0), length_block)

    stride = math.gcd(all_rows, 8)

    def forward(block_index):
        query_block, passages, length_block = block_inputs(block_index * stride, stride)
        totals = token_terms(query_block, passages, length_block)[1]
        ratio = totals / length_block[:, :, None].astype(jnp.float32)
        return jnp.sum(jnp.log(ratio), axis=2) / SHARPNESS

    slot_scores = lax.map(forward, jnp.arange(all_rows // stride)).reshape(all_rows, slot_cap)
    dense = jnp.sum(jnp.where(matches, slot_scores[:, None, :], 0.0), axis=2)
    own_scores = lax.psum_scatter(dense, "owner", scatter_dimension=0, tiled=True)
    divergence, grad_own = loss_terms(own_scores, teacher)
    grad_rows = lax.all_gather(grad_own, "owner", axis=0, tiled=True)
    slot_grads = jnp.sum(jnp.where(matches, grad_rows[:, :, None], 0.0), axis=1)
    groups = lax.axis_size("owner")
    inner = math.gcd(all_rows, 8)

    def one_block(block_index):
        first_row = 0 + block_index * inner
        query_block, passages, length_block = block_inputs(first_row, inner)
        grad_block = lax.dynamic_slice_in_dim(slot_grads, first_row, inner, 0)
        exp_terms, totals = token_terms(query_block, passages, length_block)
        weights = (exp_terms / totals[:, :, :, None]).astype(jnp.bfloat16)
        mixed = jnp.einsum("bkit,bktd->bkid", weights, passages, preferred_element_type=jnp.float32)
        return jnp.einsum("bk,bkid->bid", grad_block, mixed, precision=lax.Precision.HIGHEST)

    partials = (
        lax.map(one_block, jnp.arange(all_rows // inner))
        .reshape(all_rows, tok_count, feature)
        .reshape(groups, own_rows, tok_count, feature)
    )
    arrived = lax.all_to_all(partials, "owner", split_axis=0, concat_axis=0, tiled=True)
    unit_grad = jnp.sum(arrived, axis=0)
    radial = jnp.sum(unit_query * unit_grad, axis=-1, keepdims=True)
    query_grad = (unit_grad - unit_query * radial) * inv_norm
    return (query_grad, divergence)


def local_all(queries, pool, lengths, candidates, owner_map, teacher):
    own, toks, feat = queries.shape
    rows = pool.shape[1]
    nb = lax.axis_size("batch")
    n_rows = nb * lax.axis_size("owner")
    lanes = own * toks
    o, b = lax.axis_index("owner"), lax.axis_index("batch")
    where = jnp.stack([o, b, o * nb + b]).astype(jnp.int32)
    f32 = jnp.float32
    block = pl.pallas_call(
        norm_kernel,
        out_shape=jax.ShapeDtypeStruct(pool.shape, jnp.bfloat16),
        in_specs=[SMEM, SMEM, VMEM],
        out_specs=VMEM,
        name="norm",
    )(where, lengths, pool)
    prepared = pl.pallas_call(
        functools.partial(prep_kernel, n_rows),
        out_shape=[
            jax.ShapeDtypeStruct((feat, lanes), f32),
            jax.ShapeDtypeStruct((feat, lanes), jnp.bfloat16),
            jax.ShapeDtypeStruct((1, lanes), f32),
            jax.ShapeDtypeStruct((n_rows, lanes), f32),
            jax.ShapeDtypeStruct((n_rows, lanes), f32),
            jax.ShapeDtypeStruct((2, lanes), f32),
        ],
        in_specs=[SMEM, SMEM, SMEM, SMEM, VMEM],
        out_specs=[VMEM] * 6,
        name="prep",
    )(where, candidates, owner_map, teacher, queries)
    pieces = gather_pool(block)
    grad, div = pl.pallas_call(
        functools.partial(score_kernel, [tuple(o) for _, o in pieces], toks),
        out_shape=[jax.ShapeDtypeStruct((lanes, feat), f32), jax.ShapeDtypeStruct((1, lanes), f32)],
        in_specs=[VMEM] * (6 + len(pieces)),
        out_specs=[VMEM] * 2,
        scratch_shapes=[
            pltpu.VMEM((n_rows, rows, lanes), f32),
            pltpu.VMEM((n_rows, lanes), f32),
            pltpu.VMEM((n_rows, lanes), f32),
            pltpu.VMEM((feat, lanes), f32),
        ],
        name="score",
    )(*prepared, *[v for v, _ in pieces])
    return grad.reshape(own, toks, feat), div.reshape(own, toks)[:, 0]


def local(queries, pool, lengths, candidates, owner_map, teacher):
    own, toks = queries.shape[:2]
    n_rows = lax.axis_size("batch") * lax.axis_size("owner")
    held = n_rows * pool.shape[1] * (4 * own * toks + 2 * pool.shape[2])
    plan = local_all if held <= VMEM_BUDGET else local_by_owner
    return plan(queries, pool, lengths, candidates, owner_map, teacher)


def solution(mesh):
    in_specs = (
        P(("batch", "owner"), None, None),
        P(("owner", "batch"), None, None),
        P("owner"),
        P("batch", None),
        P(),
        P(("batch", "owner"), None),
    )
    out_specs = (P(("batch", "owner"), None, None), P(("batch", "owner")))
    return jax.shard_map(local, mesh=mesh, in_specs=in_specs, out_specs=out_specs, check_vma=False)
```

```python
import functools
import math

import jax
import jax.numpy as jnp
from jax import lax
from jax.experimental import pallas as pl
from jax.experimental.pallas import tpu as pltpu
from jax.sharding import PartitionSpec as P


SHARPNESS = 20.0
STUDENT_GAIN = 2.0
LOSS_SCALE = 64.0
EPSILON = 1e-06
LOG2E = math.log2(math.e)


VMEM_BUDGET = 24 << 20
STAGES = ((0,), (1,), (2,), (3, 4), (5,))
VMEM = pl.BlockSpec(memory_space=pltpu.VMEM)
SMEM = pl.BlockSpec(memory_space=pltpu.SMEM)


def norm_kernel(lengths_ref, pool_ref, out_ref):
    rows = pool_ref.shape[1]
    widened = pool_ref[0].astype(jnp.float32)
    inv = lax.rsqrt(jnp.sum(widened * widened, axis=-1, keepdims=True) + EPSILON)
    length = lengths_ref[lax.axis_index("batch")].astype(jnp.float32)
    last = lax.broadcasted_iota(jnp.int32, widened.shape, 0) == rows - 1
    out_ref[0] = jnp.where(last, length, widened * inv).astype(jnp.bfloat16)


def prep_kernel(order, cand_ref, map_ref, teacher_ref, query_ref,
                unit_ref, sent_ref, inv_ref, live_ref, target_ref, base_ref):
    own, toks, feat = query_ref.shape
    lanes = own * toks
    n_rows = len(order)
    qt = query_ref[...].reshape(lanes, feat).astype(jnp.float32).T
    inv = lax.rsqrt(jnp.sum(qt * qt, axis=0, keepdims=True) + EPSILON)
    unit = qt * inv
    unit_ref[...] = unit
    sent_ref[...] = unit.astype(jnp.bfloat16)
    inv_ref[...] = inv
    ncand = cand_ref.shape[1]
    group = lax.axis_index("owner")
    first = group * own
    me = group * lax.axis_size("batch") + lax.axis_index("batch")
    query_of = lax.broadcasted_iota(jnp.int32, (1, lanes), 1) // toks

    def spread(values):
        row = jnp.full((1, lanes), values[-1])
        for q in range(own - 1):
            row = jnp.where(query_of == q, values[q], row)
        return row

    teachers = [spread([teacher_ref[q, k] for q in range(own)]) for k in range(ncand)]
    log_total = jnp.log(sum(jnp.exp(t) for t in teachers))
    number = lax.broadcasted_iota(jnp.int32, (n_rows, lanes), 0)
    live = jnp.zeros((n_rows, lanes), jnp.float32)
    target = jnp.zeros((n_rows, lanes), jnp.float32)
    base = jnp.zeros((1, lanes), jnp.float32)
    mass = jnp.zeros((1, lanes), jnp.float32)
    for k in range(ncand):
        log_target = teachers[k] - log_total
        share = jnp.exp(log_target)
        base += share * log_target
        mass += share
        slot = spread([map_ref[cand_ref[first + q, k]] ^ me for q in range(own)])
        hit = number == slot
        live = jnp.where(hit, 1.0, live)
        target = jnp.where(hit, share, target)
    for place, delta in enumerate(order):
        live_ref[place:place + 1, :] = live[delta:delta + 1, :]
        target_ref[place:place + 1, :] = target[delta:delta + 1, :]
    base_ref[0:1, :] = base
    base_ref[1:2, :] = mass


def score_kernel(counts, start, toks, first, final, *refs):
    refs = list(refs)
    pieces = [refs.pop(0) for _ in counts]
    sent_ref, live_ref, target_ref = refs[:3]
    refs = refs[3:]
    if not first:
        told_ref, sums_in_ref = refs[:2]
        refs = refs[2:]
    if final:
        unit_ref, inv_ref, base_ref = refs[:3]
        refs = refs[3:]
        grad_ref, div_ref = refs[:2]
    else:
        told_out_ref, sums_ref = refs[:2]
    e_ref, tot_ref, cnt_ref = refs[2:]
    rows, lanes = e_ref.shape[1:]
    n = sum(counts)
    sent = sent_ref[...]
    token = lax.broadcasted_iota(jnp.int32, (rows, lanes), 0).astype(jnp.float32)
    where = [(ref, i) for ref, count in zip(pieces, counts) for i in range(count)]

    for j, (ref, i) in enumerate(where):
        block = ref[i]
        length = block[rows - 8:, :].astype(jnp.float32)[7:8, :]
        similar = jnp.dot(block, sent, preferred_element_type=jnp.float32)
        terms = jnp.where(token < length, jnp.exp2(similar * (SHARPNESS * LOG2E)), 0.0)
        e_ref[j] = terms
        tot_ref[j:j + 1, :] = jnp.sum(terms, axis=0, keepdims=True)
        cnt_ref[j:j + 1, :] = length

    totals = tot_ref[...]
    logs = jnp.log(totals / cnt_ref[...])
    same = (lax.broadcasted_iota(jnp.int32, (lanes, lanes), 0) // toks
            == lax.broadcasted_iota(jnp.int32, (lanes, lanes), 1) // toks).astype(jnp.float32)
    student = (STUDENT_GAIN / SHARPNESS) * jnp.dot(
        logs, same, precision=lax.Precision.HIGHEST, preferred_element_type=jnp.float32)
    target = target_ref[start:start + n, :]
    weight = live_ref[start:start + n, :] * jnp.exp(student)
    z = jnp.sum(weight, axis=0, keepdims=True)
    fit = jnp.sum(target * student, axis=0, keepdims=True)
    inverse = 1.0 / totals
    if first:
        told = jnp.zeros((2,) + sent.shape, jnp.float32)
        by_student, by_teacher = told[0], told[1]
    else:
        by_student, by_teacher = told_ref[0], told_ref[1]
        z += sums_in_ref[0:1, :]
        fit += sums_in_ref[1:2, :]

    for j, (ref, i) in enumerate(where):
        weights = (e_ref[j] * inverse[j:j + 1, :]).astype(jnp.bfloat16)
        mixed = lax.dot_general(ref[i], weights, (((0,), (0,)), ((), ())), preferred_element_type=jnp.float32)
        by_student += mixed * weight[j:j + 1, :]
        by_teacher += mixed * target[j:j + 1, :]

    if not final:
        told_out_ref[0] = by_student
        told_out_ref[1] = by_teacher
        sums_ref[0:1, :] = z
        sums_ref[1:2, :] = fit
        return
    unit_grad = (LOSS_SCALE * STUDENT_GAIN) * (by_student / z - by_teacher)
    unit = unit_ref[...]
    radial = jnp.sum(unit * unit_grad, axis=0, keepdims=True)
    out = (unit_grad - unit * radial) * inv_ref[...]
    grad_ref[...] = out.T
    div = base_ref[0:1, :] - fit + base_ref[1:2, :] * jnp.log(z)
    own = div_ref.shape[1]
    pick = (lax.broadcasted_iota(jnp.int32, (lanes, own), 0)
            == lax.broadcasted_iota(jnp.int32, (lanes, own), 1) * toks).astype(jnp.float32)
    div_ref[...] = jnp.dot(div, pick, precision=lax.Precision.HIGHEST, preferred_element_type=jnp.float32)


def exchange(value, axes, masks):
    sizes = [lax.axis_size(a) for a in axes]
    total = math.prod(sizes)

    def partner(i):
        out, rest = 0, i
        places = []
        for size in reversed(sizes):
            places.append(rest % size)
            rest //= size
        for place, size, mask in zip(reversed(places), sizes, masks):
            out = out * size + (place ^ mask)
        return out

    return lax.ppermute(value, axes if len(axes) > 1 else axes[0], [(i, partner(i)) for i in range(total)])


def gather_pool(block):
    nb, no = lax.axis_size("batch"), lax.axis_size("owner")
    far = [(("batch",), (1 << bit,), 1 << bit) for bit in range(1, nb.bit_length() - 1)]
    far += [(("owner",), (1 << bit,), nb << bit) for bit in range(2, no.bit_length() - 1)]
    near = [(("batch",), (1,), 1), (("owner",), (2,), 2 * nb), (("batch", "owner"), (1, 2), 2 * nb + 1)]

    def move(piece, step):
        axes, masks, delta = step
        return exchange(piece[0], axes, masks), [d ^ delta for d in piece[1]]

    def join(*pieces):
        return jnp.concatenate([v for v, _ in pieces], axis=0), [d for _, o in pieces for d in o]

    over = (("owner",), (1,), nb)
    held = (block, [0])
    for step in far[:-1]:
        held = join(held, move(held, step))
    rest = move(held, far[-1])
    beside = [move(held, step) for step in near]
    last = [move(rest, step) for step in near]
    mine = [held, rest]
    return [mine, beside, [move(join(*mine), over)], [move(join(*beside), over)], last, [move(join(*last), over)]]


def unit_rows(values):
    widened = values.astype(jnp.float32)
    inv_norm = lax.rsqrt(jnp.sum(widened * widened, axis=-1, keepdims=True) + EPSILON)
    return (widened * inv_norm, inv_norm)


def token_terms(query_block, passages, length_block):
    similar = jnp.einsum(
        "bid,bktd->bkit", query_block, passages, preferred_element_type=jnp.float32
    )
    in_range = lax.broadcasted_iota(jnp.int32, similar.shape, 3) < length_block[:, :, None, None]
    exp_terms = jnp.where(in_range, jnp.exp(SHARPNESS * similar), 0.0)
    return (exp_terms, jnp.sum(exp_terms, axis=3))


def loss_terms(scores, teacher_rows):
    student = STUDENT_GAIN * scores
    log_student = student - jnp.log(jnp.sum(jnp.exp(student), axis=1, keepdims=True))
    log_target = teacher_rows - jnp.log(jnp.sum(jnp.exp(teacher_rows), axis=1, keepdims=True))
    target = jnp.exp(log_target)
    divergence = jnp.sum(target * (log_target - log_student), axis=1)
    score_grad = LOSS_SCALE * STUDENT_GAIN * (jnp.exp(log_student) - target)
    return (divergence, score_grad)


def local_by_owner(queries, pool, lengths, candidates, owner_map, teacher):
    own_rows = queries.shape[0]
    all_rows = candidates.shape[0]
    tok_count = queries.shape[1]
    feature = queries.shape[2]
    slot_cap = 2 * (candidates.shape[1] // lax.axis_size("owner"))
    my_group = lax.axis_index("owner")
    unit_query, inv_norm = unit_rows(queries)
    sent_query = unit_query.astype(jnp.bfloat16)
    gathered = lax.all_gather(sent_query, "owner", axis=0, tiled=True)
    shard_unit = unit_rows(pool)[0].astype(jnp.bfloat16)
    cached = lax.all_gather(shard_unit, "batch", axis=0, tiled=True)
    group_rows = cached.shape[0]
    slot_ids = jnp.take(owner_map, candidates, axis=0)
    local_slot = slot_ids - my_group * group_rows
    is_local = (local_slot >= 0) & (local_slot < group_rows)
    order_rank = jnp.cumsum(is_local.astype(jnp.int32), axis=1) - 1
    slot_iota = lax.broadcasted_iota(jnp.int32, (1, 1, slot_cap), 2)
    matches = is_local[:, :, None] & (order_rank[:, :, None] == slot_iota)
    filled = jnp.any(matches, axis=1)
    pick_slot = jnp.sum(jnp.where(matches, local_slot[:, :, None], 0), axis=1)
    length_of = jnp.where(filled, jnp.take(lengths, pick_slot, axis=0), 1)

    def block_inputs(first_row, row_span):
        query_block = lax.dynamic_slice_in_dim(gathered, first_row, row_span, 0)
        pick_block = lax.dynamic_slice_in_dim(pick_slot, first_row, row_span, 0)
        length_block = lax.dynamic_slice_in_dim(length_of, first_row, row_span, 0)
        return (query_block, jnp.take(cached, pick_block, axis=0), length_block)

    stride = math.gcd(all_rows, 8)

    def forward(block_index):
        query_block, passages, length_block = block_inputs(block_index * stride, stride)
        totals = token_terms(query_block, passages, length_block)[1]
        ratio = totals / length_block[:, :, None].astype(jnp.float32)
        return jnp.sum(jnp.log(ratio), axis=2) / SHARPNESS

    slot_scores = lax.map(forward, jnp.arange(all_rows // stride)).reshape(all_rows, slot_cap)
    dense = jnp.sum(jnp.where(matches, slot_scores[:, None, :], 0.0), axis=2)
    own_scores = lax.psum_scatter(dense, "owner", scatter_dimension=0, tiled=True)
    divergence, grad_own = loss_terms(own_scores, teacher)
    grad_rows = lax.all_gather(grad_own, "owner", axis=0, tiled=True)
    slot_grads = jnp.sum(jnp.where(matches, grad_rows[:, :, None], 0.0), axis=1)
    groups = lax.axis_size("owner")
    inner = math.gcd(all_rows, 8)

    def one_block(block_index):
        first_row = 0 + block_index * inner
        query_block, passages, length_block = block_inputs(first_row, inner)
        grad_block = lax.dynamic_slice_in_dim(slot_grads, first_row, inner, 0)
        exp_terms, totals = token_terms(query_block, passages, length_block)
        weights = (exp_terms / totals[:, :, :, None]).astype(jnp.bfloat16)
        mixed = jnp.einsum("bkit,bktd->bkid", weights, passages, preferred_element_type=jnp.float32)
        return jnp.einsum("bk,bkid->bid", grad_block, mixed, precision=lax.Precision.HIGHEST)

    partials = (
        lax.map(one_block, jnp.arange(all_rows // inner))
        .reshape(all_rows, tok_count, feature)
        .reshape(groups, own_rows, tok_count, feature)
    )
    arrived = lax.all_to_all(partials, "owner", split_axis=0, concat_axis=0, tiled=True)
    unit_grad = jnp.sum(arrived, axis=0)
    radial = jnp.sum(unit_query * unit_grad, axis=-1, keepdims=True)
    query_grad = (unit_grad - unit_query * radial) * inv_norm
    return (query_grad, divergence)


def in_vmem(*values):
    return [pltpu.with_memory_space_constraint(v, pltpu.VMEM) for v in values]


def local_all(queries, pool, lengths, candidates, owner_map, teacher):
    own, toks, feat = queries.shape
    rows = pool.shape[1]
    lanes = own * toks
    f32 = jnp.float32
    block = pl.pallas_call(
        norm_kernel,
        out_shape=pltpu.VMEM(pool.shape, jnp.bfloat16),
        in_specs=[SMEM, VMEM],
        out_specs=VMEM,
        name="norm",
    )(lengths, pool)
    arrivals = gather_pool(block)
    stages = [sum((arrivals[i] for i in members), []) for members in STAGES]
    order = [d for stage in stages for _, offs in stage for d in offs]
    unit, sent, inv, live, target, base = pl.pallas_call(
        functools.partial(prep_kernel, order),
        out_shape=[
            pltpu.VMEM((feat, lanes), f32),
            pltpu.VMEM((feat, lanes), jnp.bfloat16),
            pltpu.VMEM((1, lanes), f32),
            pltpu.VMEM((len(order), lanes), f32),
            pltpu.VMEM((len(order), lanes), f32),
            pltpu.VMEM((2, lanes), f32),
        ],
        in_specs=[SMEM, SMEM, SMEM, VMEM],
        out_specs=[VMEM] * 6,
        name="prep",
    )(candidates, owner_map, teacher, queries)
    carry, start = (), 0
    for number, stage in enumerate(stages):
        counts = tuple(len(offs) for _, offs in stage)
        n = sum(counts)
        final = number == len(stages) - 1
        operands = [v for v, _ in stage] + [sent, live, target, *carry] + ([unit, inv, base] if final else [])
        if final:
            out_shape = [jax.ShapeDtypeStruct((lanes, feat), f32), jax.ShapeDtypeStruct((1, own), f32)]
        else:
            out_shape = [pltpu.VMEM((2, feat, lanes), f32), pltpu.VMEM((2, lanes), f32)]
        carry = pl.pallas_call(
            functools.partial(score_kernel, counts, start, toks, number == 0, final),
            out_shape=out_shape,
            in_specs=[VMEM] * len(operands),
            out_specs=[VMEM] * 2,
            scratch_shapes=[
                pltpu.VMEM((n, rows, lanes), f32),
                pltpu.VMEM((n, lanes), f32),
                pltpu.VMEM((n, lanes), f32),
            ],
        )(*in_vmem(*operands))
        start += n
    grad, div = carry
    return grad.reshape(own, toks, feat), div.reshape(own)


def local(queries, pool, lengths, candidates, owner_map, teacher):
    own, toks = queries.shape[:2]
    n_rows = lax.axis_size("batch") * lax.axis_size("owner")
    held = n_rows * pool.shape[1] * (4 * own * toks + 2 * pool.shape[2])
    plan = local_all if held <= VMEM_BUDGET else local_by_owner
    return plan(queries, pool, lengths, candidates, owner_map, teacher)


def solution(mesh):
    in_specs = (
        P(("batch", "owner"), None, None),
        P(("owner", "batch"), None, None),
        P("owner"),
        P("batch", None),
        P(),
        P(("batch", "owner"), None),
    )
    out_specs = (P(("batch", "owner"), None, None), P(("batch", "owner")))
    return jax.shard_map(local, mesh=mesh, in_specs=in_specs, out_specs=out_specs, check_vma=False)
```

```python
import functools
import math

import jax
import jax.numpy as jnp
from jax import lax
from jax.experimental import pallas as pl
from jax.experimental.pallas import tpu as pltpu
from jax.sharding import PartitionSpec as P


SHARPNESS = 20.0
STUDENT_GAIN = 2.0
LOSS_SCALE = 64.0
EPSILON = 1e-06
LOG2E = math.log2(math.e)


VMEM_BUDGET = 24 << 20
STAGES = ((0,), (1,), (2,), (3, 4, 5), (6,))
VMEM = pl.BlockSpec(memory_space=pltpu.VMEM)
SMEM = pl.BlockSpec(memory_space=pltpu.SMEM)


def norm_kernel(lengths_ref, pool_ref, out_ref):
    rows = pool_ref.shape[1]
    widened = pool_ref[0].astype(jnp.float32)
    inv = lax.rsqrt(jnp.sum(widened * widened, axis=-1, keepdims=True) + EPSILON)
    length = lengths_ref[lax.axis_index("batch")].astype(jnp.float32)
    last = lax.broadcasted_iota(jnp.int32, widened.shape, 0) == rows - 1
    out_ref[0] = jnp.where(last, length, widened * inv).astype(jnp.bfloat16)


def prep_kernel(order, cand_ref, map_ref, teacher_ref, query_ref,
                unit_ref, sent_ref, inv_ref, live_ref, target_ref, base_ref):
    own, toks, feat = query_ref.shape
    lanes = own * toks
    n_rows = len(order)
    f32 = jnp.float32
    qt = query_ref[...].reshape(lanes, feat).astype(f32).T
    inv = lax.rsqrt(jnp.sum(qt * qt, axis=0, keepdims=True) + EPSILON)
    unit = qt * inv
    unit_ref[...] = unit
    sent_ref[...] = unit.astype(jnp.bfloat16)
    inv_ref[...] = inv
    group = lax.axis_index("owner")
    me = group * lax.axis_size("batch") + lax.axis_index("batch")

    def by_lane(table, first):
        row = lax.broadcasted_iota(jnp.int32, (table.shape[0], lanes), 0)
        lane = lax.broadcasted_iota(jnp.int32, (table.shape[0], lanes), 1)
        pick = (row == lane // toks + first).astype(f32)
        return lax.dot_general(table, pick, (((0,), (0,)), ((), ())),
                               precision=lax.Precision.HIGHEST, preferred_element_type=f32)

    wanted = by_lane(cand_ref[...].astype(f32), group * own).astype(jnp.int32)
    teachers = by_lane(teacher_ref[...], 0)
    log_target = teachers - jnp.log(jnp.sum(jnp.exp(teachers), axis=0, keepdims=True))
    share = jnp.exp(log_target)
    base_ref[0:1, :] = jnp.sum(share * log_target, axis=0, keepdims=True)
    base_ref[1:2, :] = jnp.sum(share, axis=0, keepdims=True)
    passage = lax.broadcasted_iota(jnp.int32, (n_rows, lanes), 0)
    live = jnp.zeros((n_rows, lanes), f32)
    target = jnp.zeros((n_rows, lanes), f32)
    for k in range(wanted.shape[0]):
        hit = passage == wanted[k:k + 1, :]
        live = jnp.where(hit, 1.0, live)
        target = jnp.where(hit, share[k:k + 1, :], target)
    place = lax.broadcasted_iota(jnp.int32, (n_rows, n_rows), 0)
    delta = jnp.zeros((n_rows, n_rows), jnp.int32)
    for number, value in enumerate(order):
        delta = jnp.where(place == number, value, delta)
    move = (map_ref[...] == (delta ^ me)).astype(f32)
    both = jnp.dot(move, jnp.concatenate([live, target], axis=1),
                   precision=lax.Precision.HIGHEST, preferred_element_type=f32)
    live_ref[...] = both[:, :lanes]
    target_ref[...] = both[:, lanes:]


def score_kernel(counts, start, toks, first, final, *refs):
    refs = list(refs)
    pieces = [refs.pop(0) for _ in counts]
    sent_ref, live_ref, target_ref = refs[:3]
    refs = refs[3:]
    if not first:
        told_ref, sums_in_ref = refs[:2]
        refs = refs[2:]
    if final:
        unit_ref, inv_ref, base_ref = refs[:3]
        refs = refs[3:]
        grad_ref, div_ref = refs[:2]
    else:
        told_out_ref, sums_ref = refs[:2]
    e_ref, tot_ref, cnt_ref = refs[2:]
    rows, lanes = e_ref.shape[1:]
    n = sum(counts)
    sent = sent_ref[...]
    token = lax.broadcasted_iota(jnp.int32, (rows, lanes), 0).astype(jnp.float32)
    where = [(ref, i) for ref, count in zip(pieces, counts) for i in range(count)]

    for j, (ref, i) in enumerate(where):
        block = ref[i]
        length = block[rows - 8:, :].astype(jnp.float32)[7:8, :]
        similar = jnp.dot(block, sent, preferred_element_type=jnp.float32)
        terms = jnp.where(token < length, jnp.exp2(similar * (SHARPNESS * LOG2E)), 0.0)
        e_ref[j] = terms
        tot_ref[j:j + 1, :] = jnp.sum(terms, axis=0, keepdims=True)
        cnt_ref[j:j + 1, :] = length

    totals = tot_ref[...]
    logs = jnp.log(totals / cnt_ref[...])
    same = (lax.broadcasted_iota(jnp.int32, (lanes, lanes), 0) // toks
            == lax.broadcasted_iota(jnp.int32, (lanes, lanes), 1) // toks).astype(jnp.float32)
    student = (STUDENT_GAIN / SHARPNESS) * jnp.dot(
        logs, same, precision=lax.Precision.HIGHEST, preferred_element_type=jnp.float32)
    target = target_ref[start:start + n, :]
    weight = live_ref[start:start + n, :] * jnp.exp(student)
    z = jnp.sum(weight, axis=0, keepdims=True)
    fit = jnp.sum(target * student, axis=0, keepdims=True)
    inverse = 1.0 / totals
    if first:
        told = jnp.zeros((2,) + sent.shape, jnp.float32)
        by_student, by_teacher = told[0], told[1]
    else:
        by_student, by_teacher = told_ref[0], told_ref[1]
        z += sums_in_ref[0:1, :]
        fit += sums_in_ref[1:2, :]

    for j, (ref, i) in enumerate(where):
        weights = (e_ref[j] * inverse[j:j + 1, :]).astype(jnp.bfloat16)
        mixed = lax.dot_general(ref[i], weights, (((0,), (0,)), ((), ())), preferred_element_type=jnp.float32)
        by_student += mixed * weight[j:j + 1, :]
        by_teacher += mixed * target[j:j + 1, :]

    if not final:
        told_out_ref[0] = by_student
        told_out_ref[1] = by_teacher
        sums_ref[0:1, :] = z
        sums_ref[1:2, :] = fit
        return
    unit_grad = (LOSS_SCALE * STUDENT_GAIN) * (by_student / z - by_teacher)
    unit = unit_ref[...]
    radial = jnp.sum(unit * unit_grad, axis=0, keepdims=True)
    out = (unit_grad - unit * radial) * inv_ref[...]
    grad_ref[...] = out.T
    div = base_ref[0:1, :] - fit + base_ref[1:2, :] * jnp.log(z)
    own = div_ref.shape[1]
    pick = (lax.broadcasted_iota(jnp.int32, (lanes, own), 0)
            == lax.broadcasted_iota(jnp.int32, (lanes, own), 1) * toks).astype(jnp.float32)
    div_ref[...] = jnp.dot(div, pick, precision=lax.Precision.HIGHEST, preferred_element_type=jnp.float32)


def exchange(value, axes, masks):
    sizes = [lax.axis_size(a) for a in axes]
    total = math.prod(sizes)

    def partner(i):
        out, rest = 0, i
        places = []
        for size in reversed(sizes):
            places.append(rest % size)
            rest //= size
        for place, size, mask in zip(reversed(places), sizes, masks):
            out = out * size + (place ^ mask)
        return out

    return lax.ppermute(value, axes if len(axes) > 1 else axes[0], [(i, partner(i)) for i in range(total)])


def gather_pool(block):
    nb, no = lax.axis_size("batch"), lax.axis_size("owner")
    far = [(("batch",), (1 << bit,), 1 << bit) for bit in range(1, nb.bit_length() - 1)]
    far += [(("owner",), (1 << bit,), nb << bit) for bit in range(2, no.bit_length() - 1)]
    near = [(("batch",), (1,), 1), (("owner",), (2,), 2 * nb), (("batch", "owner"), (1, 2), 2 * nb + 1)]

    def move(piece, step):
        axes, masks, delta = step
        return exchange(piece[0], axes, masks), [d ^ delta for d in piece[1]]

    def both(one, two):
        return one[0], (one[1][0] ^ two[1][0],), one[2] ^ two[2]

    def join(*pieces):
        return jnp.concatenate([v for v, _ in pieces], axis=0), [d for _, o in pieces for d in o]

    over = (("owner",), (1,), nb)
    held = (block, [0])
    low, high = (far + [None, None])[:2]
    first = move(held, low)
    second = move(held, high)
    third = move(held, both(low, high))
    held = join(held, first)
    rest = join(second, third)
    beside = [move(held, step) for step in near]
    last = [move(rest, step) for step in near]
    mine = [held, rest]
    return [
        mine,
        beside,
        [move(join(*mine), over)],
        [move(join(*beside), over)],
        last,
        [move(join(*last[:2]), over)],
        [move(last[2], over)],
    ]


def unit_rows(values):
    widened = values.astype(jnp.float32)
    inv_norm = lax.rsqrt(jnp.sum(widened * widened, axis=-1, keepdims=True) + EPSILON)
    return (widened * inv_norm, inv_norm)


def token_terms(query_block, passages, length_block):
    similar = jnp.einsum(
        "bid,bktd->bkit", query_block, passages, preferred_element_type=jnp.float32
    )
    in_range = lax.broadcasted_iota(jnp.int32, similar.shape, 3) < length_block[:, :, None, None]
    exp_terms = jnp.where(in_range, jnp.exp(SHARPNESS * similar), 0.0)
    return (exp_terms, jnp.sum(exp_terms, axis=3))


def loss_terms(scores, teacher_rows):
    student = STUDENT_GAIN * scores
    log_student = student - jnp.log(jnp.sum(jnp.exp(student), axis=1, keepdims=True))
    log_target = teacher_rows - jnp.log(jnp.sum(jnp.exp(teacher_rows), axis=1, keepdims=True))
    target = jnp.exp(log_target)
    divergence = jnp.sum(target * (log_target - log_student), axis=1)
    score_grad = LOSS_SCALE * STUDENT_GAIN * (jnp.exp(log_student) - target)
    return (divergence, score_grad)


def local_by_owner(queries, pool, lengths, candidates, owner_map, teacher):
    own_rows = queries.shape[0]
    all_rows = candidates.shape[0]
    tok_count = queries.shape[1]
    feature = queries.shape[2]
    slot_cap = 2 * (candidates.shape[1] // lax.axis_size("owner"))
    my_group = lax.axis_index("owner")
    unit_query, inv_norm = unit_rows(queries)
    sent_query = unit_query.astype(jnp.bfloat16)
    gathered = lax.all_gather(sent_query, "owner", axis=0, tiled=True)
    shard_unit = unit_rows(pool)[0].astype(jnp.bfloat16)
    cached = lax.all_gather(shard_unit, "batch", axis=0, tiled=True)
    group_rows = cached.shape[0]
    slot_ids = jnp.take(owner_map, candidates, axis=0)
    local_slot = slot_ids - my_group * group_rows
    is_local = (local_slot >= 0) & (local_slot < group_rows)
    order_rank = jnp.cumsum(is_local.astype(jnp.int32), axis=1) - 1
    slot_iota = lax.broadcasted_iota(jnp.int32, (1, 1, slot_cap), 2)
    matches = is_local[:, :, None] & (order_rank[:, :, None] == slot_iota)
    filled = jnp.any(matches, axis=1)
    pick_slot = jnp.sum(jnp.where(matches, local_slot[:, :, None], 0), axis=1)
    length_of = jnp.where(filled, jnp.take(lengths, pick_slot, axis=0), 1)

    def block_inputs(first_row, row_span):
        query_block = lax.dynamic_slice_in_dim(gathered, first_row, row_span, 0)
        pick_block = lax.dynamic_slice_in_dim(pick_slot, first_row, row_span, 0)
        length_block = lax.dynamic_slice_in_dim(length_of, first_row, row_span, 0)
        return (query_block, jnp.take(cached, pick_block, axis=0), length_block)

    stride = math.gcd(all_rows, 8)

    def forward(block_index):
        query_block, passages, length_block = block_inputs(block_index * stride, stride)
        totals = token_terms(query_block, passages, length_block)[1]
        ratio = totals / length_block[:, :, None].astype(jnp.float32)
        return jnp.sum(jnp.log(ratio), axis=2) / SHARPNESS

    slot_scores = lax.map(forward, jnp.arange(all_rows // stride)).reshape(all_rows, slot_cap)
    dense = jnp.sum(jnp.where(matches, slot_scores[:, None, :], 0.0), axis=2)
    own_scores = lax.psum_scatter(dense, "owner", scatter_dimension=0, tiled=True)
    divergence, grad_own = loss_terms(own_scores, teacher)
    grad_rows = lax.all_gather(grad_own, "owner", axis=0, tiled=True)
    slot_grads = jnp.sum(jnp.where(matches, grad_rows[:, :, None], 0.0), axis=1)
    groups = lax.axis_size("owner")
    inner = math.gcd(all_rows, 8)

    def one_block(block_index):
        first_row = 0 + block_index * inner
        query_block, passages, length_block = block_inputs(first_row, inner)
        grad_block = lax.dynamic_slice_in_dim(slot_grads, first_row, inner, 0)
        exp_terms, totals = token_terms(query_block, passages, length_block)
        weights = (exp_terms / totals[:, :, :, None]).astype(jnp.bfloat16)
        mixed = jnp.einsum("bkit,bktd->bkid", weights, passages, preferred_element_type=jnp.float32)
        return jnp.einsum("bk,bkid->bid", grad_block, mixed, precision=lax.Precision.HIGHEST)

    partials = (
        lax.map(one_block, jnp.arange(all_rows // inner))
        .reshape(all_rows, tok_count, feature)
        .reshape(groups, own_rows, tok_count, feature)
    )
    arrived = lax.all_to_all(partials, "owner", split_axis=0, concat_axis=0, tiled=True)
    unit_grad = jnp.sum(arrived, axis=0)
    radial = jnp.sum(unit_query * unit_grad, axis=-1, keepdims=True)
    query_grad = (unit_grad - unit_query * radial) * inv_norm
    return (query_grad, divergence)


def in_vmem(*values):
    return [pltpu.with_memory_space_constraint(v, pltpu.VMEM) for v in values]


def local_all(queries, pool, lengths, candidates, owner_map, teacher):
    own, toks, feat = queries.shape
    rows = pool.shape[1]
    lanes = own * toks
    f32 = jnp.float32
    block = pl.pallas_call(
        norm_kernel,
        out_shape=pltpu.VMEM(pool.shape, jnp.bfloat16),
        in_specs=[SMEM, VMEM],
        out_specs=VMEM,
        name="norm",
    )(lengths, pool)
    arrivals = gather_pool(block)
    stages = [sum((arrivals[i] for i in members), []) for members in STAGES]
    order = [d for stage in stages for _, offs in stage for d in offs]
    unit, sent, inv, live, target, base = pl.pallas_call(
        functools.partial(prep_kernel, order),
        out_shape=[
            pltpu.VMEM((feat, lanes), f32),
            pltpu.VMEM((feat, lanes), jnp.bfloat16),
            pltpu.VMEM((1, lanes), f32),
            pltpu.VMEM((len(order), lanes), f32),
            pltpu.VMEM((len(order), lanes), f32),
            pltpu.VMEM((2, lanes), f32),
        ],
        in_specs=[VMEM] * 4,
        out_specs=[VMEM] * 6,
        name="prep",
    )(*in_vmem(candidates, owner_map.reshape(1, -1), teacher, queries))
    carry, start = (), 0
    for number, stage in enumerate(stages):
        counts = tuple(len(offs) for _, offs in stage)
        n = sum(counts)
        final = number == len(stages) - 1
        operands = [v for v, _ in stage] + [sent, live, target, *carry] + ([unit, inv, base] if final else [])
        if final:
            out_shape = [jax.ShapeDtypeStruct((lanes, feat), f32), jax.ShapeDtypeStruct((1, own), f32)]
        else:
            out_shape = [pltpu.VMEM((2, feat, lanes), f32), pltpu.VMEM((2, lanes), f32)]
        carry = pl.pallas_call(
            functools.partial(score_kernel, counts, start, toks, number == 0, final),
            out_shape=out_shape,
            in_specs=[VMEM] * len(operands),
            out_specs=[VMEM] * 2,
            scratch_shapes=[
                pltpu.VMEM((n, rows, lanes), f32),
                pltpu.VMEM((n, lanes), f32),
                pltpu.VMEM((n, lanes), f32),
            ],
        )(*in_vmem(*operands))
        start += n
    grad, div = carry
    return grad.reshape(own, toks, feat), div.reshape(own)


def local(queries, pool, lengths, candidates, owner_map, teacher):
    own, toks = queries.shape[:2]
    n_rows = lax.axis_size("batch") * lax.axis_size("owner")
    held = n_rows * pool.shape[1] * (4 * own * toks + 2 * pool.shape[2])
    plan = local_all if held <= VMEM_BUDGET else local_by_owner
    return plan(queries, pool, lengths, candidates, owner_map, teacher)


def solution(mesh):
    in_specs = (
        P(("batch", "owner"), None, None),
        P(("owner", "batch"), None, None),
        P("owner"),
        P("batch", None),
        P(),
        P(("batch", "owner"), None),
    )
    out_specs = (P(("batch", "owner"), None, None), P(("batch", "owner")))
    return jax.shard_map(local, mesh=mesh, in_specs=in_specs, out_specs=out_specs, check_vma=False)
```

```python
import functools
import math

import jax
import jax.numpy as jnp
from jax import lax
from jax.experimental import pallas as pl
from jax.experimental.pallas import tpu as pltpu
from jax.sharding import PartitionSpec as P


SHARPNESS = 20.0
STUDENT_GAIN = 2.0
LOSS_SCALE = 64.0
EPSILON = 1e-06
LOG2E = math.log2(math.e)


VMEM_BUDGET = 24 << 20
COST = 1 << 24
VMEM = pl.BlockSpec(memory_space=pltpu.VMEM)
SMEM = pl.BlockSpec(memory_space=pltpu.SMEM)


def norm_kernel(masks, lengths_ref, *refs):
    out_ref = refs[-1]
    rows = out_ref.shape[1]
    lengths = lengths_ref[...].astype(jnp.float32)
    place = lax.broadcasted_iota(jnp.int32, lengths.shape, 1)
    last = lax.broadcasted_iota(jnp.int32, out_ref.shape[1:], 0) == rows - 1
    for i, (mask, ref) in enumerate(zip(masks, refs)):
        widened = ref[0].astype(jnp.float32)
        inv = lax.rsqrt(jnp.sum(widened * widened, axis=-1, keepdims=True) + EPSILON)
        theirs = place == lax.axis_index("batch") ^ mask
        length = jnp.sum(jnp.where(theirs, lengths, 0.0), axis=1, keepdims=True)
        out_ref[i] = jnp.where(last, length, widened * inv).astype(jnp.bfloat16)


def order_kernel(order, out_ref):
    me = lax.axis_index("owner") * lax.axis_size("batch") + lax.axis_index("batch")
    place = lax.broadcasted_iota(jnp.int32, out_ref.shape, 0)
    row = jnp.zeros(out_ref.shape, jnp.int32)
    for number, delta in enumerate(order):
        row = jnp.where(place == number, delta, row)
    out_ref[...] = row ^ me


def prep_kernel(order_ref, cand_ref, map_ref, teacher_ref, query_ref,
                unit_ref, sent_ref, inv_ref, live_ref, target_ref, base_ref):
    own, toks, feat = query_ref.shape
    lanes = own * toks
    n_rows = order_ref.shape[0]
    f32 = jnp.float32
    qt = query_ref[...].reshape(lanes, feat).astype(f32).T
    inv = lax.rsqrt(jnp.sum(qt * qt, axis=0, keepdims=True) + EPSILON)
    unit = qt * inv
    unit_ref[...] = unit
    sent_ref[...] = unit.astype(jnp.bfloat16)
    inv_ref[...] = inv
    group = lax.axis_index("owner")

    def by_lane(table, first):
        row = lax.broadcasted_iota(jnp.int32, (table.shape[0], lanes), 0)
        lane = lax.broadcasted_iota(jnp.int32, (table.shape[0], lanes), 1)
        pick = (row == lane // toks + first).astype(f32)
        return lax.dot_general(table, pick, (((0,), (0,)), ((), ())),
                               precision=lax.Precision.HIGHEST, preferred_element_type=f32)

    wanted = by_lane(cand_ref[...].astype(f32), group * own).astype(jnp.int32)
    teachers = by_lane(teacher_ref[...], 0)
    log_target = teachers - jnp.log(jnp.sum(jnp.exp(teachers), axis=0, keepdims=True))
    share = jnp.exp(log_target)
    base_ref[0:1, :] = jnp.sum(share * log_target, axis=0, keepdims=True)
    base_ref[1:2, :] = jnp.sum(share, axis=0, keepdims=True)
    passage = lax.broadcasted_iota(jnp.int32, (n_rows, lanes), 0)
    live = jnp.zeros((n_rows, lanes), f32)
    target = jnp.zeros((n_rows, lanes), f32)
    for k in range(wanted.shape[0]):
        hit = passage == wanted[k:k + 1, :]
        live = jnp.where(hit, 1.0, live)
        target = jnp.where(hit, share[k:k + 1, :], target)
    move = (map_ref[...] == order_ref[...]).astype(f32)
    both = jnp.dot(move, jnp.concatenate([live, target], axis=1),
                   precision=lax.Precision.HIGHEST, preferred_element_type=f32)
    live_ref[...] = both[:, :lanes]
    target_ref[...] = both[:, lanes:]


def exact_dot(values, picks):
    parts = []
    for _ in range(3):
        parts.append(values.astype(jnp.bfloat16))
        values = values - parts[-1].astype(jnp.float32)
    return jnp.dot(jnp.concatenate(parts, axis=1), jnp.concatenate([picks] * 3, axis=0),
                   preferred_element_type=jnp.float32)


def score_kernel(counts, start, toks, first, final, *refs):
    refs = list(refs)
    pieces = [refs.pop(0) for _ in counts]
    sent_ref, live_ref, target_ref = refs[:3]
    refs = refs[3:]
    if not first:
        told_ref, sums_in_ref = refs[:2]
        refs = refs[2:]
    if final:
        unit_ref, inv_ref, base_ref = refs[:3]
        refs = refs[3:]
        grad_ref, div_ref = refs[:2]
    else:
        told_out_ref, sums_ref = refs[:2]
    e_ref, tot_ref, cnt_ref = refs[2:]
    rows, lanes = e_ref.shape[1:]
    n = sum(counts)
    sent = sent_ref[...]
    token = lax.broadcasted_iota(jnp.int32, (rows, lanes), 0).astype(jnp.float32)
    where = [(ref, i) for ref, count in zip(pieces, counts) for i in range(count)]

    for j, (ref, i) in enumerate(where):
        block = ref[i]
        length = block[rows - 8:, :].astype(jnp.float32)[7:8, :]
        similar = jnp.dot(block, sent, preferred_element_type=jnp.float32)
        terms = jnp.where(token < length, jnp.exp2(similar * (SHARPNESS * LOG2E)), 0.0)
        e_ref[j] = terms
        tot_ref[j:j + 1, :] = jnp.sum(terms, axis=0, keepdims=True)
        cnt_ref[j:j + 1, :] = length

    totals = tot_ref[...]
    logs = jnp.log(totals / cnt_ref[...])
    same = (lax.broadcasted_iota(jnp.int32, (lanes, lanes), 0) // toks
            == lax.broadcasted_iota(jnp.int32, (lanes, lanes), 1) // toks).astype(jnp.bfloat16)
    student = (STUDENT_GAIN / SHARPNESS) * exact_dot(logs, same)
    target = target_ref[start:start + n, :]
    weight = live_ref[start:start + n, :] * jnp.exp(student)
    z = jnp.sum(weight, axis=0, keepdims=True)
    fit = jnp.sum(target * student, axis=0, keepdims=True)
    inverse = 1.0 / totals
    if first:
        told = jnp.zeros((2,) + sent.shape, jnp.float32)
        by_student, by_teacher = told[0], told[1]
    else:
        by_student, by_teacher = told_ref[0], told_ref[1]
        z += sums_in_ref[0:1, :]
        fit += sums_in_ref[1:2, :]

    for j, (ref, i) in enumerate(where):
        weights = (e_ref[j] * inverse[j:j + 1, :]).astype(jnp.bfloat16)
        mixed = lax.dot_general(ref[i], weights, (((0,), (0,)), ((), ())), preferred_element_type=jnp.float32)
        by_student += mixed * weight[j:j + 1, :]
        by_teacher += mixed * target[j:j + 1, :]

    if not final:
        told_out_ref[0] = by_student
        told_out_ref[1] = by_teacher
        sums_ref[0:1, :] = z
        sums_ref[1:2, :] = fit
        return
    scale = LOSS_SCALE * STUDENT_GAIN
    unit_grad = by_student * (scale / z) - scale * by_teacher
    unit = unit_ref[...]
    radial = jnp.sum(unit * unit_grad, axis=0, keepdims=True)
    out = (unit_grad - unit * radial) * inv_ref[...]
    grad_ref[...] = out.T
    div = base_ref[0:1, :] - fit + base_ref[1:2, :] * jnp.log(z)
    own = div_ref.shape[1]
    pick = (lax.broadcasted_iota(jnp.int32, (lanes, own), 0)
            == lax.broadcasted_iota(jnp.int32, (lanes, own), 1) * toks).astype(jnp.bfloat16)
    div_ref[...] = exact_dot(div, pick)


def exchange(piece, db, do):
    nb, no = lax.axis_size("batch"), lax.axis_size("owner")
    pairs = [(b * no + o, (b ^ db) * no + (o ^ do)) for b in range(nb) for o in range(no)]
    value = lax.ppermute(piece[0], ("batch", "owner"), pairs)
    return value, [d ^ db ^ nb * do for d in piece[1]]


def gather_pool(pool, normalize):
    nb = lax.axis_size("batch")
    masks = [2] + list(range(nb - 2, 2, -2))
    raw = [exchange((pool, [0]), mask, 0)[0] for mask in masks]
    held = normalize([0, masks[0]], [pool, raw[0]])
    rest = normalize(masks[1:], raw[1:])
    near = ((1, 0), (0, 2), (1, 2))
    beside = [exchange(held, *way) for way in near]
    last = [exchange(rest, *way) for way in near]
    mine = [held, rest]

    def over(*pieces):
        value = jnp.concatenate([v for v, _ in pieces], axis=0) if len(pieces) > 1 else pieces[0][0]
        return exchange((value, [d for _, o in pieces for d in o]), 0, 1)

    return [[*mine, *beside], [over(*mine)], [over(*beside), *last[:2]], [last[2], over(*last[:2])], [over(last[2])]]


def unit_rows(values):
    widened = values.astype(jnp.float32)
    inv_norm = lax.rsqrt(jnp.sum(widened * widened, axis=-1, keepdims=True) + EPSILON)
    return (widened * inv_norm, inv_norm)


def token_terms(query_block, passages, length_block):
    similar = jnp.einsum(
        "bid,bktd->bkit", query_block, passages, preferred_element_type=jnp.float32
    )
    in_range = lax.broadcasted_iota(jnp.int32, similar.shape, 3) < length_block[:, :, None, None]
    exp_terms = jnp.where(in_range, jnp.exp(SHARPNESS * similar), 0.0)
    return (exp_terms, jnp.sum(exp_terms, axis=3))


def loss_terms(scores, teacher_rows):
    student = STUDENT_GAIN * scores
    log_student = student - jnp.log(jnp.sum(jnp.exp(student), axis=1, keepdims=True))
    log_target = teacher_rows - jnp.log(jnp.sum(jnp.exp(teacher_rows), axis=1, keepdims=True))
    target = jnp.exp(log_target)
    divergence = jnp.sum(target * (log_target - log_student), axis=1)
    score_grad = LOSS_SCALE * STUDENT_GAIN * (jnp.exp(log_student) - target)
    return (divergence, score_grad)


def local_by_owner(queries, pool, lengths, candidates, owner_map, teacher):
    own_rows = queries.shape[0]
    all_rows = candidates.shape[0]
    tok_count = queries.shape[1]
    feature = queries.shape[2]
    slot_cap = 2 * (candidates.shape[1] // lax.axis_size("owner"))
    my_group = lax.axis_index("owner")
    unit_query, inv_norm = unit_rows(queries)
    sent_query = unit_query.astype(jnp.bfloat16)
    gathered = lax.all_gather(sent_query, "owner", axis=0, tiled=True)
    shard_unit = unit_rows(pool)[0].astype(jnp.bfloat16)
    cached = lax.all_gather(shard_unit, "batch", axis=0, tiled=True)
    group_rows = cached.shape[0]
    slot_ids = jnp.take(owner_map, candidates, axis=0)
    local_slot = slot_ids - my_group * group_rows
    is_local = (local_slot >= 0) & (local_slot < group_rows)
    order_rank = jnp.cumsum(is_local.astype(jnp.int32), axis=1) - 1
    slot_iota = lax.broadcasted_iota(jnp.int32, (1, 1, slot_cap), 2)
    matches = is_local[:, :, None] & (order_rank[:, :, None] == slot_iota)
    filled = jnp.any(matches, axis=1)
    pick_slot = jnp.sum(jnp.where(matches, local_slot[:, :, None], 0), axis=1)
    length_of = jnp.where(filled, jnp.take(lengths, pick_slot, axis=0), 1)

    def block_inputs(first_row, row_span):
        query_block = lax.dynamic_slice_in_dim(gathered, first_row, row_span, 0)
        pick_block = lax.dynamic_slice_in_dim(pick_slot, first_row, row_span, 0)
        length_block = lax.dynamic_slice_in_dim(length_of, first_row, row_span, 0)
        return (query_block, jnp.take(cached, pick_block, axis=0), length_block)

    stride = math.gcd(all_rows, 8)

    def forward(block_index):
        query_block, passages, length_block = block_inputs(block_index * stride, stride)
        totals = token_terms(query_block, passages, length_block)[1]
        ratio = totals / length_block[:, :, None].astype(jnp.float32)
        return jnp.sum(jnp.log(ratio), axis=2) / SHARPNESS

    slot_scores = lax.map(forward, jnp.arange(all_rows // stride)).reshape(all_rows, slot_cap)
    dense = jnp.sum(jnp.where(matches, slot_scores[:, None, :], 0.0), axis=2)
    own_scores = lax.psum_scatter(dense, "owner", scatter_dimension=0, tiled=True)
    divergence, grad_own = loss_terms(own_scores, teacher)
    grad_rows = lax.all_gather(grad_own, "owner", axis=0, tiled=True)
    slot_grads = jnp.sum(jnp.where(matches, grad_rows[:, :, None], 0.0), axis=1)
    groups = lax.axis_size("owner")
    inner = math.gcd(all_rows, 8)

    def one_block(block_index):
        first_row = 0 + block_index * inner
        query_block, passages, length_block = block_inputs(first_row, inner)
        grad_block = lax.dynamic_slice_in_dim(slot_grads, first_row, inner, 0)
        exp_terms, totals = token_terms(query_block, passages, length_block)
        weights = (exp_terms / totals[:, :, :, None]).astype(jnp.bfloat16)
        mixed = jnp.einsum("bkit,bktd->bkid", weights, passages, preferred_element_type=jnp.float32)
        return jnp.einsum("bk,bkid->bid", grad_block, mixed, precision=lax.Precision.HIGHEST)

    partials = (
        lax.map(one_block, jnp.arange(all_rows // inner))
        .reshape(all_rows, tok_count, feature)
        .reshape(groups, own_rows, tok_count, feature)
    )
    arrived = lax.all_to_all(partials, "owner", split_axis=0, concat_axis=0, tiled=True)
    unit_grad = jnp.sum(arrived, axis=0)
    radial = jnp.sum(unit_query * unit_grad, axis=-1, keepdims=True)
    query_grad = (unit_grad - unit_query * radial) * inv_norm
    return (query_grad, divergence)


def in_vmem(*values):
    return [pltpu.with_memory_space_constraint(v, pltpu.VMEM) for v in values]


def local_all(queries, pool, lengths, candidates, owner_map, teacher):
    own, toks, feat = queries.shape
    rows = pool.shape[1]
    lanes = own * toks
    f32 = jnp.float32

    def normalize(masks, blocks):
        value = pl.pallas_call(
            functools.partial(norm_kernel, masks),
            out_shape=pltpu.VMEM((len(masks), rows, feat), jnp.bfloat16),
            in_specs=[VMEM] * (1 + len(masks)),
            out_specs=VMEM,
            name="norm",
        )(*in_vmem(lengths.reshape(1, -1), *blocks))
        return value, list(masks)

    stages = gather_pool(pool, normalize)
    order = [d for stage in stages for _, offs in stage for d in offs]
    numbers = pl.pallas_call(
        functools.partial(order_kernel, order),
        out_shape=pltpu.VMEM((len(order), len(order)), jnp.int32),
        out_specs=VMEM,
        cost_estimate=pl.CostEstimate(flops=COST, bytes_accessed=COST, transcendentals=0),
        name="order",
    )()
    unit, sent, inv, live, target, base = pl.pallas_call(
        prep_kernel,
        out_shape=[
            pltpu.VMEM((feat, lanes), f32),
            pltpu.VMEM((feat, lanes), jnp.bfloat16),
            pltpu.VMEM((1, lanes), f32),
            pltpu.VMEM((len(order), lanes), f32),
            pltpu.VMEM((len(order), lanes), f32),
            pltpu.VMEM((2, lanes), f32),
        ],
        in_specs=[VMEM] * 5,
        out_specs=[VMEM] * 6,
        name="prep",
    )(*in_vmem(numbers, candidates, owner_map.reshape(1, -1), teacher, queries))
    carry, start = (), 0
    for number, stage in enumerate(stages):
        counts = tuple(value.shape[0] for value, _ in stage)
        n = sum(counts)
        final = number == len(stages) - 1
        operands = [v for v, _ in stage] + [sent, live, target, *carry] + ([unit, inv, base] if final else [])
        if final:
            out_shape = [jax.ShapeDtypeStruct((lanes, feat), f32), jax.ShapeDtypeStruct((1, own), f32)]
        else:
            out_shape = [pltpu.VMEM((2, feat, lanes), f32), pltpu.VMEM((2, lanes), f32)]
        carry = pl.pallas_call(
            functools.partial(score_kernel, counts, start, toks, number == 0, final),
            out_shape=out_shape,
            in_specs=[VMEM] * len(operands),
            out_specs=[VMEM] * 2,
            scratch_shapes=[
                pltpu.VMEM((n, rows, lanes), f32),
                pltpu.VMEM((n, lanes), f32),
                pltpu.VMEM((n, lanes), f32),
            ],
        )(*in_vmem(*operands))
        start += n
    grad, div = carry
    return grad.reshape(own, toks, feat), div.reshape(own)


def local(queries, pool, lengths, candidates, owner_map, teacher):
    own, toks = queries.shape[:2]
    n_rows = lax.axis_size("batch") * lax.axis_size("owner")
    held = n_rows * pool.shape[1] * (4 * own * toks + 2 * pool.shape[2])
    nb = lax.axis_size("batch")
    paired = nb >= 8 and nb & (nb - 1) == 0 and lax.axis_size("owner") == 4
    plan = local_all if paired and held <= VMEM_BUDGET else local_by_owner
    return plan(queries, pool, lengths, candidates, owner_map, teacher)


def solution(mesh):
    in_specs = (
        P(("batch", "owner"), None, None),
        P(("owner", "batch"), None, None),
        P("owner"),
        P("batch", None),
        P(),
        P(("batch", "owner"), None),
    )
    out_specs = (P(("batch", "owner"), None, None), P(("batch", "owner")))
    return jax.shard_map(local, mesh=mesh, in_specs=in_specs, out_specs=out_specs, check_vma=False)
```

```python
import functools
import math

import jax
import jax.numpy as jnp
from jax import lax
from jax.experimental import pallas as pl
from jax.experimental.pallas import tpu as pltpu
from jax.sharding import PartitionSpec as P


SHARPNESS = 20.0
STUDENT_GAIN = 2.0
LOSS_SCALE = 64.0
EPSILON = 1e-06
LOG2E = math.log2(math.e)


VMEM_BUDGET = 24 << 20
COST = 1 << 24
VMEM = pl.BlockSpec(memory_space=pltpu.VMEM)
SMEM = pl.BlockSpec(memory_space=pltpu.SMEM)


def norm_kernel(masks, lengths_ref, *refs):
    out_ref = refs[-1]
    rows = out_ref.shape[1]
    lengths = lengths_ref[...].astype(jnp.float32)
    place = lax.broadcasted_iota(jnp.int32, lengths.shape, 1)
    last = lax.broadcasted_iota(jnp.int32, out_ref.shape[1:], 0) == rows - 1
    for i, (mask, ref) in enumerate(zip(masks, refs)):
        widened = ref[0].astype(jnp.float32)
        inv = lax.rsqrt(jnp.sum(widened * widened, axis=-1, keepdims=True) + EPSILON)
        theirs = place == lax.axis_index("batch") ^ mask
        length = jnp.sum(jnp.where(theirs, lengths, 0.0), axis=1, keepdims=True)
        out_ref[i] = jnp.where(last, length, widened * inv).astype(jnp.bfloat16)


def order_kernel(order, out_ref):
    me = lax.axis_index("owner") * lax.axis_size("batch") + lax.axis_index("batch")
    place = lax.broadcasted_iota(jnp.int32, out_ref.shape, 0)
    row = jnp.zeros(out_ref.shape, jnp.int32)
    odd = lax.axis_index("owner") % 2
    for number, delta in enumerate(order):
        row = jnp.where(place == number, delta[0] + odd * (delta[1] - delta[0]), row)
    out_ref[...] = row ^ me


def prep_kernel(order_ref, cand_ref, map_ref, teacher_ref, query_ref,
                unit_ref, sent_ref, inv_ref, live_ref, target_ref, base_ref):
    own, toks, feat = query_ref.shape
    lanes = own * toks
    n_rows = order_ref.shape[0]
    f32 = jnp.float32
    qt = query_ref[...].reshape(lanes, feat).astype(f32).T
    inv = lax.rsqrt(jnp.sum(qt * qt, axis=0, keepdims=True) + EPSILON)
    unit = qt * inv
    unit_ref[...] = unit
    sent_ref[...] = unit.astype(jnp.bfloat16)
    inv_ref[...] = inv
    group = lax.axis_index("owner")

    def by_lane(table, first):
        row = lax.broadcasted_iota(jnp.int32, (table.shape[0], lanes), 0)
        lane = lax.broadcasted_iota(jnp.int32, (table.shape[0], lanes), 1)
        pick = (row == lane // toks + first).astype(f32)
        return lax.dot_general(table, pick, (((0,), (0,)), ((), ())),
                               precision=lax.Precision.HIGHEST, preferred_element_type=f32)

    wanted = by_lane(cand_ref[...].astype(f32), group * own).astype(jnp.int32)
    teachers = by_lane(teacher_ref[...], 0)
    log_target = teachers - jnp.log(jnp.sum(jnp.exp(teachers), axis=0, keepdims=True))
    share = jnp.exp(log_target)
    base_ref[0:1, :] = jnp.sum(share * log_target, axis=0, keepdims=True)
    base_ref[1:2, :] = jnp.sum(share, axis=0, keepdims=True)
    passage = lax.broadcasted_iota(jnp.int32, (n_rows, lanes), 0)
    live = jnp.zeros((n_rows, lanes), f32)
    target = jnp.zeros((n_rows, lanes), f32)
    for k in range(wanted.shape[0]):
        hit = passage == wanted[k:k + 1, :]
        live = jnp.where(hit, 1.0, live)
        target = jnp.where(hit, share[k:k + 1, :], target)
    move = (map_ref[...] == order_ref[...]).astype(f32)
    both = jnp.dot(move, jnp.concatenate([live, target], axis=1),
                   precision=lax.Precision.HIGHEST, preferred_element_type=f32)
    live_ref[...] = both[:, :lanes]
    target_ref[...] = both[:, lanes:]


def exact_dot(values, picks):
    parts = []
    for _ in range(3):
        parts.append(values.astype(jnp.bfloat16))
        values = values - parts[-1].astype(jnp.float32)
    return jnp.dot(jnp.concatenate(parts, axis=1), jnp.concatenate([picks] * 3, axis=0),
                   preferred_element_type=jnp.float32)


def score_kernel(counts, start, toks, first, final, *refs):
    refs = list(refs)
    pieces = [refs.pop(0) for _ in counts]
    sent_ref, live_ref, target_ref = refs[:3]
    refs = refs[3:]
    if not first:
        told_ref, sums_in_ref = refs[:2]
        refs = refs[2:]
    if final:
        unit_ref, inv_ref, base_ref = refs[:3]
        refs = refs[3:]
        grad_ref, div_ref = refs[:2]
    else:
        told_out_ref, sums_ref = refs[:2]
    e_ref, tot_ref, cnt_ref = refs[2:]
    rows, lanes = e_ref.shape[1:]
    n = sum(counts)
    sent = sent_ref[...]
    token = lax.broadcasted_iota(jnp.int32, (rows, lanes), 0).astype(jnp.float32)
    where = [(ref, i) for ref, count in zip(pieces, counts) for i in range(count)]

    for j, (ref, i) in enumerate(where):
        block = ref[i]
        length = block[rows - 8:, :].astype(jnp.float32)[7:8, :]
        similar = jnp.dot(block, sent, preferred_element_type=jnp.float32)
        terms = jnp.where(token < length, jnp.exp2(similar * (SHARPNESS * LOG2E)), 0.0)
        e_ref[j] = terms
        tot_ref[j:j + 1, :] = jnp.sum(terms, axis=0, keepdims=True)
        cnt_ref[j:j + 1, :] = length

    totals = tot_ref[...]
    logs = jnp.log(totals / cnt_ref[...])
    same = (lax.broadcasted_iota(jnp.int32, (lanes, lanes), 0) // toks
            == lax.broadcasted_iota(jnp.int32, (lanes, lanes), 1) // toks).astype(jnp.bfloat16)
    student = (STUDENT_GAIN / SHARPNESS) * exact_dot(logs, same)
    target = target_ref[start:start + n, :]
    weight = live_ref[start:start + n, :] * jnp.exp(student)
    z = jnp.sum(weight, axis=0, keepdims=True)
    fit = jnp.sum(target * student, axis=0, keepdims=True)
    inverse = 1.0 / totals
    if first:
        told = jnp.zeros((2,) + sent.shape, jnp.float32)
        by_student, by_teacher = told[0], told[1]
    else:
        by_student, by_teacher = told_ref[0], told_ref[1]
        z += sums_in_ref[0:1, :]
        fit += sums_in_ref[1:2, :]

    for j, (ref, i) in enumerate(where):
        weights = (e_ref[j] * inverse[j:j + 1, :]).astype(jnp.bfloat16)
        mixed = lax.dot_general(ref[i], weights, (((0,), (0,)), ((), ())), preferred_element_type=jnp.float32)
        by_student += mixed * weight[j:j + 1, :]
        by_teacher += mixed * target[j:j + 1, :]

    if not final:
        told_out_ref[0] = by_student
        told_out_ref[1] = by_teacher
        sums_ref[0:1, :] = z
        sums_ref[1:2, :] = fit
        return
    scale = LOSS_SCALE * STUDENT_GAIN
    unit_grad = by_student * (scale / z) - scale * by_teacher
    unit = unit_ref[...]
    radial = jnp.sum(unit * unit_grad, axis=0, keepdims=True)
    out = (unit_grad - unit * radial) * inv_ref[...]
    grad_ref[...] = out.T
    div = base_ref[0:1, :] - fit + base_ref[1:2, :] * jnp.log(z)
    own = div_ref.shape[1]
    pick = (lax.broadcasted_iota(jnp.int32, (lanes, own), 0)
            == lax.broadcasted_iota(jnp.int32, (lanes, own), 1) * toks).astype(jnp.bfloat16)
    div_ref[...] = exact_dot(div, pick)


def exchange(piece, *ways):
    nb, no = lax.axis_size("batch"), lax.axis_size("owner")
    ways = ways * (2 // len(ways))
    pairs = [(b * no + o, (b ^ ways[o % 2][0]) * no + (o ^ ways[o % 2][1])) for b in range(nb) for o in range(no)]
    value = lax.ppermute(piece[0], ("batch", "owner"), pairs)
    even, odd = (db ^ nb * do for db, do in ways)
    swapped = ways[0][1] % 2
    return value, [(q ^ even, p ^ odd) if swapped else (p ^ even, q ^ odd) for p, q in piece[1]]


def gather_pool(pool, normalize):
    nb = lax.axis_size("batch")
    masks = [2] + list(range(nb - 2, 2, -2))
    raw = [exchange((pool, [(0, 0)]), (mask, 0))[0] for mask in masks]
    held = normalize([0, masks[0]], [pool, raw[0]])
    rest = normalize(masks[1:], raw[1:])
    near = (((1, 2), (1, 0)), ((1, 0), (0, 2)), ((0, 2), (1, 2)))
    beside = [exchange(held, *way) for way in near]
    last = [exchange(rest, *way) for way in near]
    mine = [held, rest]

    def over(*pieces):
        value = jnp.concatenate([v for v, _ in pieces], axis=0) if len(pieces) > 1 else pieces[0][0]
        return exchange((value, [d for _, o in pieces for d in o]), (0, 1))

    return [[*mine, *beside], [over(*mine), over(*beside)], last, [over(*last[:2])], [over(last[2])]]


def unit_rows(values):
    widened = values.astype(jnp.float32)
    inv_norm = lax.rsqrt(jnp.sum(widened * widened, axis=-1, keepdims=True) + EPSILON)
    return (widened * inv_norm, inv_norm)


def token_terms(query_block, passages, length_block):
    similar = jnp.einsum(
        "bid,bktd->bkit", query_block, passages, preferred_element_type=jnp.float32
    )
    in_range = lax.broadcasted_iota(jnp.int32, similar.shape, 3) < length_block[:, :, None, None]
    exp_terms = jnp.where(in_range, jnp.exp(SHARPNESS * similar), 0.0)
    return (exp_terms, jnp.sum(exp_terms, axis=3))


def loss_terms(scores, teacher_rows):
    student = STUDENT_GAIN * scores
    log_student = student - jnp.log(jnp.sum(jnp.exp(student), axis=1, keepdims=True))
    log_target = teacher_rows - jnp.log(jnp.sum(jnp.exp(teacher_rows), axis=1, keepdims=True))
    target = jnp.exp(log_target)
    divergence = jnp.sum(target * (log_target - log_student), axis=1)
    score_grad = LOSS_SCALE * STUDENT_GAIN * (jnp.exp(log_student) - target)
    return (divergence, score_grad)


def local_by_owner(queries, pool, lengths, candidates, owner_map, teacher):
    own_rows = queries.shape[0]
    all_rows = candidates.shape[0]
    tok_count = queries.shape[1]
    feature = queries.shape[2]
    slot_cap = 2 * (candidates.shape[1] // lax.axis_size("owner"))
    my_group = lax.axis_index("owner")
    unit_query, inv_norm = unit_rows(queries)
    sent_query = unit_query.astype(jnp.bfloat16)
    gathered = lax.all_gather(sent_query, "owner", axis=0, tiled=True)
    shard_unit = unit_rows(pool)[0].astype(jnp.bfloat16)
    cached = lax.all_gather(shard_unit, "batch", axis=0, tiled=True)
    group_rows = cached.shape[0]
    slot_ids = jnp.take(owner_map, candidates, axis=0)
    local_slot = slot_ids - my_group * group_rows
    is_local = (local_slot >= 0) & (local_slot < group_rows)
    order_rank = jnp.cumsum(is_local.astype(jnp.int32), axis=1) - 1
    slot_iota = lax.broadcasted_iota(jnp.int32, (1, 1, slot_cap), 2)
    matches = is_local[:, :, None] & (order_rank[:, :, None] == slot_iota)
    filled = jnp.any(matches, axis=1)
    pick_slot = jnp.sum(jnp.where(matches, local_slot[:, :, None], 0), axis=1)
    length_of = jnp.where(filled, jnp.take(lengths, pick_slot, axis=0), 1)

    def block_inputs(first_row, row_span):
        query_block = lax.dynamic_slice_in_dim(gathered, first_row, row_span, 0)
        pick_block = lax.dynamic_slice_in_dim(pick_slot, first_row, row_span, 0)
        length_block = lax.dynamic_slice_in_dim(length_of, first_row, row_span, 0)
        return (query_block, jnp.take(cached, pick_block, axis=0), length_block)

    stride = math.gcd(all_rows, 8)

    def forward(block_index):
        query_block, passages, length_block = block_inputs(block_index * stride, stride)
        totals = token_terms(query_block, passages, length_block)[1]
        ratio = totals / length_block[:, :, None].astype(jnp.float32)
        return jnp.sum(jnp.log(ratio), axis=2) / SHARPNESS

    slot_scores = lax.map(forward, jnp.arange(all_rows // stride)).reshape(all_rows, slot_cap)
    dense = jnp.sum(jnp.where(matches, slot_scores[:, None, :], 0.0), axis=2)
    own_scores = lax.psum_scatter(dense, "owner", scatter_dimension=0, tiled=True)
    divergence, grad_own = loss_terms(own_scores, teacher)
    grad_rows = lax.all_gather(grad_own, "owner", axis=0, tiled=True)
    slot_grads = jnp.sum(jnp.where(matches, grad_rows[:, :, None], 0.0), axis=1)
    groups = lax.axis_size("owner")
    inner = math.gcd(all_rows, 8)

    def one_block(block_index):
        first_row = 0 + block_index * inner
        query_block, passages, length_block = block_inputs(first_row, inner)
        grad_block = lax.dynamic_slice_in_dim(slot_grads, first_row, inner, 0)
        exp_terms, totals = token_terms(query_block, passages, length_block)
        weights = (exp_terms / totals[:, :, :, None]).astype(jnp.bfloat16)
        mixed = jnp.einsum("bkit,bktd->bkid", weights, passages, preferred_element_type=jnp.float32)
        return jnp.einsum("bk,bkid->bid", grad_block, mixed, precision=lax.Precision.HIGHEST)

    partials = (
        lax.map(one_block, jnp.arange(all_rows // inner))
        .reshape(all_rows, tok_count, feature)
        .reshape(groups, own_rows, tok_count, feature)
    )
    arrived = lax.all_to_all(partials, "owner", split_axis=0, concat_axis=0, tiled=True)
    unit_grad = jnp.sum(arrived, axis=0)
    radial = jnp.sum(unit_query * unit_grad, axis=-1, keepdims=True)
    query_grad = (unit_grad - unit_query * radial) * inv_norm
    return (query_grad, divergence)


def in_vmem(*values):
    return [pltpu.with_memory_space_constraint(v, pltpu.VMEM) for v in values]


def local_all(queries, pool, lengths, candidates, owner_map, teacher):
    own, toks, feat = queries.shape
    rows = pool.shape[1]
    lanes = own * toks
    f32 = jnp.float32

    def normalize(masks, blocks):
        value = pl.pallas_call(
            functools.partial(norm_kernel, masks),
            out_shape=pltpu.VMEM((len(masks), rows, feat), jnp.bfloat16),
            in_specs=[VMEM] * (1 + len(masks)),
            out_specs=VMEM,
            name="norm",
        )(*in_vmem(lengths.reshape(1, -1), *blocks))
        return value, [(mask, mask) for mask in masks]

    stages = gather_pool(pool, normalize)
    order = [d for stage in stages for _, offs in stage for d in offs]
    numbers = pl.pallas_call(
        functools.partial(order_kernel, order),
        out_shape=pltpu.VMEM((len(order), len(order)), jnp.int32),
        out_specs=VMEM,
        cost_estimate=pl.CostEstimate(flops=COST, bytes_accessed=COST, transcendentals=0),
        name="order",
    )()
    unit, sent, inv, live, target, base = pl.pallas_call(
        prep_kernel,
        out_shape=[
            pltpu.VMEM((feat, lanes), f32),
            pltpu.VMEM((feat, lanes), jnp.bfloat16),
            pltpu.VMEM((1, lanes), f32),
            pltpu.VMEM((len(order), lanes), f32),
            pltpu.VMEM((len(order), lanes), f32),
            pltpu.VMEM((2, lanes), f32),
        ],
        in_specs=[VMEM] * 5,
        out_specs=[VMEM] * 6,
        name="prep",
    )(*in_vmem(numbers, candidates, owner_map.reshape(1, -1), teacher, queries))
    carry, start = (), 0
    for number, stage in enumerate(stages):
        counts = tuple(value.shape[0] for value, _ in stage)
        n = sum(counts)
        final = number == len(stages) - 1
        operands = [v for v, _ in stage] + [sent, live, target, *carry] + ([unit, inv, base] if final else [])
        if final:
            out_shape = [jax.ShapeDtypeStruct((lanes, feat), f32), jax.ShapeDtypeStruct((1, own), f32)]
        else:
            out_shape = [pltpu.VMEM((2, feat, lanes), f32), pltpu.VMEM((2, lanes), f32)]
        carry = pl.pallas_call(
            functools.partial(score_kernel, counts, start, toks, number == 0, final),
            out_shape=out_shape,
            in_specs=[VMEM] * len(operands),
            out_specs=[VMEM] * 2,
            scratch_shapes=[
                pltpu.VMEM((n, rows, lanes), f32),
                pltpu.VMEM((n, lanes), f32),
                pltpu.VMEM((n, lanes), f32),
            ],
        )(*in_vmem(*operands))
        start += n
    grad, div = carry
    return grad.reshape(own, toks, feat), div.reshape(own)


def local(queries, pool, lengths, candidates, owner_map, teacher):
    own, toks = queries.shape[:2]
    n_rows = lax.axis_size("batch") * lax.axis_size("owner")
    held = n_rows * pool.shape[1] * (4 * own * toks + 2 * pool.shape[2])
    nb = lax.axis_size("batch")
    paired = nb >= 8 and nb & (nb - 1) == 0 and lax.axis_size("owner") == 4
    plan = local_all if paired and held <= VMEM_BUDGET else local_by_owner
    return plan(queries, pool, lengths, candidates, owner_map, teacher)


def solution(mesh):
    in_specs = (
        P(("batch", "owner"), None, None),
        P(("owner", "batch"), None, None),
        P("owner"),
        P("batch", None),
        P(),
        P(("batch", "owner"), None),
    )
    out_specs = (P(("batch", "owner"), None, None), P(("batch", "owner")))
    return jax.shard_map(local, mesh=mesh, in_specs=in_specs, out_specs=out_specs, check_vma=False)
```

```python
import functools
import math

import jax
import jax.numpy as jnp
from jax import lax
from jax.experimental import pallas as pl
from jax.experimental.pallas import tpu as pltpu
from jax.sharding import PartitionSpec as P


SHARPNESS = 20.0
STUDENT_GAIN = 2.0
LOSS_SCALE = 64.0
EPSILON = 1e-06
LOG2E = math.log2(math.e)


VMEM_BUDGET = 24 << 20
COST = 1 << 24
VMEM = pl.BlockSpec(memory_space=pltpu.VMEM)
SMEM = pl.BlockSpec(memory_space=pltpu.SMEM)


def norm_kernel(masks, lengths_ref, *refs):
    out_ref = refs[-1]
    rows = out_ref.shape[1]
    lengths = lengths_ref[...].astype(jnp.float32)
    place = lax.broadcasted_iota(jnp.int32, lengths.shape, 1)
    last = lax.broadcasted_iota(jnp.int32, out_ref.shape[1:], 0) == rows - 1
    for i, (mask, ref) in enumerate(zip(masks, refs)):
        widened = ref[0].astype(jnp.float32)
        inv = lax.rsqrt(jnp.sum(widened * widened, axis=-1, keepdims=True) + EPSILON)
        theirs = place == lax.axis_index("batch") ^ mask
        length = jnp.sum(jnp.where(theirs, lengths, 0.0), axis=1, keepdims=True)
        out_ref[i] = jnp.where(last, length, widened * inv).astype(jnp.bfloat16)


def order_kernel(order, out_ref):
    me = lax.axis_index("owner") * lax.axis_size("batch") + lax.axis_index("batch")
    place = lax.broadcasted_iota(jnp.int32, out_ref.shape, 0)
    row = jnp.zeros(out_ref.shape, jnp.int32)
    odd = lax.axis_index("owner") % 2
    for number, delta in enumerate(order):
        row = jnp.where(place == number, delta[0] + odd * (delta[1] - delta[0]), row)
    out_ref[...] = row ^ me


def prep_kernel(order_ref, cand_ref, map_ref, teacher_ref, query_ref,
                unit_ref, sent_ref, inv_ref, live_ref, target_ref, base_ref):
    own, toks, feat = query_ref.shape
    lanes = own * toks
    n_rows = order_ref.shape[0]
    f32 = jnp.float32
    qt = query_ref[...].reshape(lanes, feat).astype(f32).T
    inv = lax.rsqrt(jnp.sum(qt * qt, axis=0, keepdims=True) + EPSILON)
    unit = qt * inv
    unit_ref[...] = unit
    sent_ref[...] = unit.astype(jnp.bfloat16)
    inv_ref[...] = inv
    group = lax.axis_index("owner")

    def by_lane(table, first):
        row = lax.broadcasted_iota(jnp.int32, (table.shape[0], lanes), 0)
        lane = lax.broadcasted_iota(jnp.int32, (table.shape[0], lanes), 1)
        pick = (row == lane // toks + first).astype(f32)
        return lax.dot_general(table, pick, (((0,), (0,)), ((), ())),
                               precision=lax.Precision.HIGHEST, preferred_element_type=f32)

    wanted = by_lane(cand_ref[...].astype(f32), group * own).astype(jnp.int32)
    teachers = by_lane(teacher_ref[...], 0)
    log_target = teachers - jnp.log(jnp.sum(jnp.exp(teachers), axis=0, keepdims=True))
    share = jnp.exp(log_target)
    base_ref[0:1, :] = jnp.sum(share * log_target, axis=0, keepdims=True)
    base_ref[1:2, :] = jnp.sum(share, axis=0, keepdims=True)
    passage = lax.broadcasted_iota(jnp.int32, (n_rows, lanes), 0)
    live = jnp.zeros((n_rows, lanes), f32)
    target = jnp.zeros((n_rows, lanes), f32)
    for k in range(wanted.shape[0]):
        hit = passage == wanted[k:k + 1, :]
        live = jnp.where(hit, 1.0, live)
        target = jnp.where(hit, share[k:k + 1, :], target)
    move = (map_ref[...] == order_ref[...]).astype(f32)
    both = jnp.dot(move, jnp.concatenate([live, target], axis=1),
                   precision=lax.Precision.HIGHEST, preferred_element_type=f32)
    live_ref[...] = both[:, :lanes]
    target_ref[...] = both[:, lanes:]


def exact_dot(values, picks):
    parts = []
    for _ in range(3):
        parts.append(values.astype(jnp.bfloat16))
        values = values - parts[-1].astype(jnp.float32)
    return jnp.dot(jnp.concatenate(parts, axis=1), jnp.concatenate([picks] * 3, axis=0),
                   preferred_element_type=jnp.float32)


def score_kernel(counts, start, toks, first, final, *refs):
    refs = list(refs)
    pieces = [refs.pop(0) for _ in counts]
    sent_ref, live_ref, target_ref = refs[:3]
    refs = refs[3:]
    if not first:
        told_ref, sums_in_ref = refs[:2]
        refs = refs[2:]
    if final:
        unit_ref, inv_ref, base_ref = refs[:3]
        refs = refs[3:]
        grad_ref, div_ref = refs[:2]
    else:
        told_out_ref, sums_ref = refs[:2]
    e_ref, tot_ref, cnt_ref = refs[2:]
    rows, lanes = e_ref.shape[1:]
    n = sum(counts)
    sent = sent_ref[...]
    token = lax.broadcasted_iota(jnp.int32, (rows, lanes), 0).astype(jnp.float32)
    where = [(ref, i) for ref, count in zip(pieces, counts) for i in range(count)]

    for j, (ref, i) in enumerate(where):
        block = ref[i]
        length = block[rows - 8:, :].astype(jnp.float32)[7:8, :]
        similar = jnp.dot(block, sent, preferred_element_type=jnp.float32)
        terms = jnp.where(token < length, jnp.exp2(similar * (SHARPNESS * LOG2E)), 0.0)
        e_ref[j] = terms
        tot_ref[j:j + 1, :] = jnp.sum(terms, axis=0, keepdims=True)
        cnt_ref[j:j + 1, :] = length

    totals = tot_ref[...]
    logs = jnp.log(totals / cnt_ref[...])
    same = (lax.broadcasted_iota(jnp.int32, (lanes, lanes), 0) // toks
            == lax.broadcasted_iota(jnp.int32, (lanes, lanes), 1) // toks).astype(jnp.bfloat16)
    student = (STUDENT_GAIN / SHARPNESS) * exact_dot(logs, same)
    target = target_ref[start:start + n, :]
    weight = live_ref[start:start + n, :] * jnp.exp(student)
    z = jnp.sum(weight, axis=0, keepdims=True)
    fit = jnp.sum(target * student, axis=0, keepdims=True)
    inverse = 1.0 / totals
    if first:
        told = jnp.zeros((2,) + sent.shape, jnp.float32)
        by_student, by_teacher = told[0], told[1]
    else:
        by_student, by_teacher = told_ref[0], told_ref[1]
        z += sums_in_ref[0:1, :]
        fit += sums_in_ref[1:2, :]

    for j, (ref, i) in enumerate(where):
        weights = (e_ref[j] * inverse[j:j + 1, :]).astype(jnp.bfloat16)
        mixed = lax.dot_general(ref[i], weights, (((0,), (0,)), ((), ())), preferred_element_type=jnp.float32)
        by_student += mixed * weight[j:j + 1, :]
        by_teacher += mixed * target[j:j + 1, :]

    if not final:
        told_out_ref[0] = by_student
        told_out_ref[1] = by_teacher
        sums_ref[0:1, :] = z
        sums_ref[1:2, :] = fit
        return
    scale = LOSS_SCALE * STUDENT_GAIN
    unit_grad = by_student * (scale / z) - scale * by_teacher
    unit = unit_ref[...]
    radial = jnp.sum(unit * unit_grad, axis=0, keepdims=True)
    out = (unit_grad - unit * radial) * inv_ref[...]
    grad_ref[...] = out.T
    div = base_ref[0:1, :] - fit + base_ref[1:2, :] * jnp.log(z)
    own = div_ref.shape[1]
    pick = (lax.broadcasted_iota(jnp.int32, (lanes, own), 0)
            == lax.broadcasted_iota(jnp.int32, (lanes, own), 1) * toks).astype(jnp.bfloat16)
    div_ref[...] = exact_dot(div, pick)


def exchange(piece, *ways):
    nb, no = lax.axis_size("batch"), lax.axis_size("owner")
    ways = ways * (2 // len(ways))
    pairs = [(b * no + o, (b ^ ways[o % 2][0]) * no + (o ^ ways[o % 2][1])) for b in range(nb) for o in range(no)]
    value = lax.ppermute(piece[0], ("batch", "owner"), pairs)
    even, odd = (db ^ nb * do for db, do in ways)
    swapped = ways[0][1] % 2
    return value, [(q ^ even, p ^ odd) if swapped else (p ^ even, q ^ odd) for p, q in piece[1]]


def gather_pool(pool, normalize):
    nb = lax.axis_size("batch")
    masks = [2] + list(range(nb - 2, 2, -2))
    raw = [exchange((pool, [(0, 0)]), (mask, 0))[0] for mask in masks]
    held = normalize([0, masks[0]], [pool, raw[0]])
    rest = normalize(masks[1:], raw[1:])
    near = (((1, 2), (0, 2)), ((1, 0), (1, 0)), ((0, 2), (1, 2)))
    plain = (((1, 0),), ((0, 2),), ((1, 2),))
    beside = [exchange(held, *way) for way in plain]
    last = [exchange(rest, *way) for way in near]
    mine = [held, rest]

    def over(*pieces):
        value = jnp.concatenate([v for v, _ in pieces], axis=0) if len(pieces) > 1 else pieces[0][0]
        return exchange((value, [d for _, o in pieces for d in o]), (0, 1))

    return [[*mine, *beside], [over(*mine), over(*beside)], last, [over(*last[:2]), over(last[2])]]


def unit_rows(values):
    widened = values.astype(jnp.float32)
    inv_norm = lax.rsqrt(jnp.sum(widened * widened, axis=-1, keepdims=True) + EPSILON)
    return (widened * inv_norm, inv_norm)


def token_terms(query_block, passages, length_block):
    similar = jnp.einsum(
        "bid,bktd->bkit", query_block, passages, preferred_element_type=jnp.float32
    )
    in_range = lax.broadcasted_iota(jnp.int32, similar.shape, 3) < length_block[:, :, None, None]
    exp_terms = jnp.where(in_range, jnp.exp(SHARPNESS * similar), 0.0)
    return (exp_terms, jnp.sum(exp_terms, axis=3))


def loss_terms(scores, teacher_rows):
    student = STUDENT_GAIN * scores
    log_student = student - jnp.log(jnp.sum(jnp.exp(student), axis=1, keepdims=True))
    log_target = teacher_rows - jnp.log(jnp.sum(jnp.exp(teacher_rows), axis=1, keepdims=True))
    target = jnp.exp(log_target)
    divergence = jnp.sum(target * (log_target - log_student), axis=1)
    score_grad = LOSS_SCALE * STUDENT_GAIN * (jnp.exp(log_student) - target)
    return (divergence, score_grad)


def local_by_owner(queries, pool, lengths, candidates, owner_map, teacher):
    own_rows = queries.shape[0]
    all_rows = candidates.shape[0]
    tok_count = queries.shape[1]
    feature = queries.shape[2]
    slot_cap = 2 * (candidates.shape[1] // lax.axis_size("owner"))
    my_group = lax.axis_index("owner")
    unit_query, inv_norm = unit_rows(queries)
    sent_query = unit_query.astype(jnp.bfloat16)
    gathered = lax.all_gather(sent_query, "owner", axis=0, tiled=True)
    shard_unit = unit_rows(pool)[0].astype(jnp.bfloat16)
    cached = lax.all_gather(shard_unit, "batch", axis=0, tiled=True)
    group_rows = cached.shape[0]
    slot_ids = jnp.take(owner_map, candidates, axis=0)
    local_slot = slot_ids - my_group * group_rows
    is_local = (local_slot >= 0) & (local_slot < group_rows)
    order_rank = jnp.cumsum(is_local.astype(jnp.int32), axis=1) - 1
    slot_iota = lax.broadcasted_iota(jnp.int32, (1, 1, slot_cap), 2)
    matches = is_local[:, :, None] & (order_rank[:, :, None] == slot_iota)
    filled = jnp.any(matches, axis=1)
    pick_slot = jnp.sum(jnp.where(matches, local_slot[:, :, None], 0), axis=1)
    length_of = jnp.where(filled, jnp.take(lengths, pick_slot, axis=0), 1)

    def block_inputs(first_row, row_span):
        query_block = lax.dynamic_slice_in_dim(gathered, first_row, row_span, 0)
        pick_block = lax.dynamic_slice_in_dim(pick_slot, first_row, row_span, 0)
        length_block = lax.dynamic_slice_in_dim(length_of, first_row, row_span, 0)
        return (query_block, jnp.take(cached, pick_block, axis=0), length_block)

    stride = math.gcd(all_rows, 8)

    def forward(block_index):
        query_block, passages, length_block = block_inputs(block_index * stride, stride)
        totals = token_terms(query_block, passages, length_block)[1]
        ratio = totals / length_block[:, :, None].astype(jnp.float32)
        return jnp.sum(jnp.log(ratio), axis=2) / SHARPNESS

    slot_scores = lax.map(forward, jnp.arange(all_rows // stride)).reshape(all_rows, slot_cap)
    dense = jnp.sum(jnp.where(matches, slot_scores[:, None, :], 0.0), axis=2)
    own_scores = lax.psum_scatter(dense, "owner", scatter_dimension=0, tiled=True)
    divergence, grad_own = loss_terms(own_scores, teacher)
    grad_rows = lax.all_gather(grad_own, "owner", axis=0, tiled=True)
    slot_grads = jnp.sum(jnp.where(matches, grad_rows[:, :, None], 0.0), axis=1)
    groups = lax.axis_size("owner")
    inner = math.gcd(all_rows, 8)

    def one_block(block_index):
        first_row = 0 + block_index * inner
        query_block, passages, length_block = block_inputs(first_row, inner)
        grad_block = lax.dynamic_slice_in_dim(slot_grads, first_row, inner, 0)
        exp_terms, totals = token_terms(query_block, passages, length_block)
        weights = (exp_terms / totals[:, :, :, None]).astype(jnp.bfloat16)
        mixed = jnp.einsum("bkit,bktd->bkid", weights, passages, preferred_element_type=jnp.float32)
        return jnp.einsum("bk,bkid->bid", grad_block, mixed, precision=lax.Precision.HIGHEST)

    partials = (
        lax.map(one_block, jnp.arange(all_rows // inner))
        .reshape(all_rows, tok_count, feature)
        .reshape(groups, own_rows, tok_count, feature)
    )
    arrived = lax.all_to_all(partials, "owner", split_axis=0, concat_axis=0, tiled=True)
    unit_grad = jnp.sum(arrived, axis=0)
    radial = jnp.sum(unit_query * unit_grad, axis=-1, keepdims=True)
    query_grad = (unit_grad - unit_query * radial) * inv_norm
    return (query_grad, divergence)


def in_vmem(*values):
    return [pltpu.with_memory_space_constraint(v, pltpu.VMEM) for v in values]


def local_all(queries, pool, lengths, candidates, owner_map, teacher):
    own, toks, feat = queries.shape
    rows = pool.shape[1]
    lanes = own * toks
    f32 = jnp.float32

    def normalize(masks, blocks):
        value = pl.pallas_call(
            functools.partial(norm_kernel, masks),
            out_shape=pltpu.VMEM((len(masks), rows, feat), jnp.bfloat16),
            in_specs=[VMEM] * (1 + len(masks)),
            out_specs=VMEM,
            name="norm",
        )(*in_vmem(lengths.reshape(1, -1), *blocks))
        return value, [(mask, mask) for mask in masks]

    stages = gather_pool(pool, normalize)
    order = [d for stage in stages for _, offs in stage for d in offs]
    numbers = pl.pallas_call(
        functools.partial(order_kernel, order),
        out_shape=pltpu.VMEM((len(order), len(order)), jnp.int32),
        out_specs=VMEM,
        cost_estimate=pl.CostEstimate(flops=COST, bytes_accessed=COST, transcendentals=0),
        name="order",
    )()
    unit, sent, inv, live, target, base = pl.pallas_call(
        prep_kernel,
        out_shape=[
            pltpu.VMEM((feat, lanes), f32),
            pltpu.VMEM((feat, lanes), jnp.bfloat16),
            pltpu.VMEM((1, lanes), f32),
            pltpu.VMEM((len(order), lanes), f32),
            pltpu.VMEM((len(order), lanes), f32),
            pltpu.VMEM((2, lanes), f32),
        ],
        in_specs=[VMEM] * 5,
        out_specs=[VMEM] * 6,
        name="prep",
    )(*in_vmem(numbers, candidates, owner_map.reshape(1, -1), teacher, queries))
    carry, start = (), 0
    for number, stage in enumerate(stages):
        counts = tuple(value.shape[0] for value, _ in stage)
        n = sum(counts)
        final = number == len(stages) - 1
        operands = [v for v, _ in stage] + [sent, live, target, *carry] + ([unit, inv, base] if final else [])
        if final:
            out_shape = [jax.ShapeDtypeStruct((lanes, feat), f32), jax.ShapeDtypeStruct((1, own), f32)]
        else:
            out_shape = [pltpu.VMEM((2, feat, lanes), f32), pltpu.VMEM((2, lanes), f32)]
        carry = pl.pallas_call(
            functools.partial(score_kernel, counts, start, toks, number == 0, final),
            out_shape=out_shape,
            in_specs=[VMEM] * len(operands),
            out_specs=[VMEM] * 2,
            scratch_shapes=[
                pltpu.VMEM((n, rows, lanes), f32),
                pltpu.VMEM((n, lanes), f32),
                pltpu.VMEM((n, lanes), f32),
            ],
        )(*in_vmem(*operands))
        start += n
    grad, div = carry
    return grad.reshape(own, toks, feat), div.reshape(own)


def local(queries, pool, lengths, candidates, owner_map, teacher):
    own, toks = queries.shape[:2]
    n_rows = lax.axis_size("batch") * lax.axis_size("owner")
    held = n_rows * pool.shape[1] * (4 * own * toks + 2 * pool.shape[2])
    nb = lax.axis_size("batch")
    paired = nb >= 8 and nb & (nb - 1) == 0 and lax.axis_size("owner") == 4
    plan = local_all if paired and held <= VMEM_BUDGET else local_by_owner
    return plan(queries, pool, lengths, candidates, owner_map, teacher)


def solution(mesh):
    in_specs = (
        P(("batch", "owner"), None, None),
        P(("owner", "batch"), None, None),
        P("owner"),
        P("batch", None),
        P(),
        P(("batch", "owner"), None),
    )
    out_specs = (P(("batch", "owner"), None, None), P(("batch", "owner")))
    return jax.shard_map(local, mesh=mesh, in_specs=in_specs, out_specs=out_specs, check_vma=False)
```
